32 devices in a mesh: groups: 2 (over y), pages: 4 (over z), patches: 4 (over x, core).
Axes of the slice: x: 2, y: 2, z: 4, core: 2. Of those that a mesh axis runs over, the one named last changes fastest.
Arguments:
- queries: bfloat16 [16, 32, 128], P(('groups', 'pages'), 'patches'), parts along dimension 0, may hold values from -6 to 6
- gallery: bfloat16 [640, 1024, 128], P(('groups', 'pages'), 'patches'), parts along dimension 0, may hold values from -0.5 to 0.5
- page_rows: int32 [640], P('groups'), parts along dimension 0, may hold values from 0 to 319, as said below
- candidates: int32 [16, 32], P(('groups', 'pages')), parts along dimension 0, may hold values from 0 to 319, as said below
Outputs:
- scores: float32 [16, 32], P(('groups', 'pages')), parts along dimension 0
The draws below stay inside these ranges and needn't reach their ends.
There are 2 independent parts, one for each index of `groups`. The reference program is written for one: setup_inputs(seed, part) draws one part's arguments, and reference() takes and returns one part's arrays. A program takes and returns all parts, laid end to end along the dimension named above; each array names one. Nothing has to cross between parts.
Inputs may be any that keep to these rules, and one draw needn't show every extreme that they name: A permutation: page id c is stored at row page_rows[c] of gallery, which lies on pages index page_rows[c] // 80. Each query's 32 page ids are distinct. The 2 queries of one pages index have at most 48 candidates stored on one pages index, and in every draw some pages index stores exactly 48 candidates of the queries of every pages index.
All inputs are finite; a program needn't handle non-finite values.
Results may differ from the reference program's by a relative error of at most 0.0003.
Values may be sent and summed in bfloat16 or wider, within the bound.
No kernel may reach another device: no remote copies, remote signals or barrier semaphores. Data moves between devices by JAX's collectives and lax.ppermute only.
A program may use at most 64 MiB of HBM per device.

```python
import jax
import jax.numpy as jnp
from jax import lax

DIM = 128
PATCH = 1024
QT = 32
CAND_OWN = 8
NQ_DEV = 2
PG_DEV = 80
CAND = 32
NQ = 8
PAGES = 320
N_PAGES = 4


def candidate_plan(key):
    owners = N_PAGES
    spots = 4 * CAND_OWN
    page_rows = jax.random.permutation(jax.random.fold_in(key, 101), PAGES).astype(jnp.int32)
    row_to_page = jnp.argsort(page_rows).astype(jnp.int32)
    hottest = jax.random.randint(jax.random.fold_in(key, 102), (), 0, owners)
    offsets = jax.random.randint(jax.random.fold_in(key, 103), (owners, NQ_DEV), 0, CAND_OWN)
    query_index = jnp.arange(NQ_DEV)
    signs = jnp.where(query_index % 2 == 0, 1, -1)
    signs = jnp.where((query_index % 2 == 0) & (query_index == NQ_DEV - 1), 0, signs)
    hot_counts = 3 * CAND_OWN + signs[None, :] * offsets[:, query_index // 2]
    limits = jax.random.randint(jax.random.fold_in(key, 104), (owners, NQ_DEV, owners), CAND_OWN, 3 * CAND_OWN + 1)
    is_hot = jnp.arange(owners) == hottest
    limits = jnp.where(is_hot[None, None, :], 0, limits)
    slot_index = jnp.arange(3 * CAND_OWN)
    open_slots = slot_index[None, None, None, :] < limits[..., None]
    noise = jax.random.randint(jax.random.fold_in(key, 105), open_slots.shape, 0, 2 ** 20)
    priority = jnp.where(open_slots, 2 ** 21, 0) + noise
    flat_priority = priority.reshape(owners, NQ_DEV, owners * 3 * CAND_OWN)
    ordering = jnp.argsort(-flat_priority, axis=-1)
    position = jnp.argsort(ordering, axis=-1)
    needed = CAND - hot_counts
    chosen = position < needed[..., None]
    counts = jnp.sum(chosen.reshape(owners, NQ_DEV, owners, 3 * CAND_OWN).astype(jnp.int32), axis=-1)
    counts = counts + jnp.where(is_hot[None, None, :], hot_counts[..., None], 0)
    local_noise = jax.random.randint(jax.random.fold_in(key, 106), (owners, NQ_DEV, owners, PG_DEV), 0, 2 ** 30)
    local_order = jnp.argsort(local_noise, axis=-1)[..., :spots].astype(jnp.int32)
    spot_index = jnp.arange(spots)
    usable = spot_index[None, None, None, :] < counts[..., None]
    storage = jnp.arange(owners, dtype=jnp.int32)[None, None, :, None] * PG_DEV + local_order
    flat_storage = storage.reshape(owners, NQ_DEV, owners * spots)
    flat_usable = usable.reshape(owners, NQ_DEV, owners * spots)
    shuffle = jax.random.randint(jax.random.fold_in(key, 107), flat_storage.shape, 0, 2 ** 20)
    sort_keys = jnp.where(flat_usable, 0, 2 ** 21) + shuffle
    taken = jnp.argsort(sort_keys, axis=-1)[..., :CAND]
    picked = jnp.take_along_axis(flat_storage, taken, axis=-1)
    candidates = row_to_page[picked].reshape(owners * NQ_DEV, CAND).astype(jnp.int32)
    return (page_rows, candidates)


def draw_page_rows(key, part):
    return candidate_plan(key)[0]


def draw_candidates(key, part):
    return candidate_plan(key)[1]


def level_of(rng, shape, shards, low, top_value):
    factor_of = 1.0
    for dim, parts in shards:
        heights = jax.random.uniform(jax.random.fold_in(jax.random.fold_in(rng, 6), dim), (parts,), jnp.float32, low / len(shards), top_value / len(shards))
        factor_of = factor_of * jnp.repeat(jnp.exp(heights), shape[dim] // parts).reshape((-1,) + (1,) * (len(shape) - 1 - dim))
    return factor_of


def centred(stream_key, extent, scale, reach, split=(), kind=jnp.bfloat16):
    drawn = jax.random.normal(stream_key, extent, jnp.float32) * scale
    if len(split) > 0:
        drawn = level_of(stream_key, extent, split, -0.22, 0.18) * drawn
    return jnp.clip(drawn, min=-reach, max=reach).astype(kind)


def setup_inputs(seed: int = 0, part: int = 0) -> dict:
    arg_keys = jax.random.split(jax.random.key(seed), 5)
    own_keys = jax.random.split(jax.random.fold_in(arg_keys[4], part), 5)
    queries = centred(own_keys[0], (NQ, QT, DIM), 1.0, 6.0, ((0, 4), (1, 4)))
    gallery = centred(own_keys[1], (PAGES, PATCH, DIM), DIM ** -0.5, 0.5, ((0, 4), (1, 4)))
    page_rows = draw_page_rows(jax.random.fold_in(jax.random.fold_in(arg_keys[4], part), 71), part)
    candidates = draw_candidates(jax.random.fold_in(jax.random.fold_in(arg_keys[4], part), 71), part)
    return dict(queries=queries, gallery=gallery, page_rows=page_rows, candidates=candidates)


def reference(queries, gallery, page_rows, candidates):
    rows = jnp.take(page_rows, candidates, axis=0).astype(jnp.int32)

    def per_query(item):
        tokens, row_ids = item
        pages = jnp.take(gallery, row_ids, axis=0).astype(jnp.float32)
        sims = jnp.einsum("td,cpd->ctp", tokens.astype(jnp.float32), pages, precision=lax.Precision.HIGHEST)
        return jnp.mean(jnp.max(sims, axis=2), axis=1)

    return lax.map(per_query, (queries, rows))
```

```python
import functools

import jax
import jax.numpy as jnp
from jax import lax
from jax.experimental import pallas as pl
from jax.experimental.pallas import tpu as pltpu
from jax.sharding import PartitionSpec as P

LANES = 128
BASE = 128
GROUP = ("pages", "patches")
VMEM = pl.BlockSpec(memory_space=pltpu.VMEM)


def lookup_kernel(candidates_ref, page_rows_ref, info_ref):
    queries, cand = candidates_ref.shape
    pages = page_rows_ref.shape[1]
    count = queries * cand
    repeat = max(1, LANES // count)
    blocks = count * repeat // LANES
    table = page_rows_ref[...].astype(jnp.float32)
    high = jnp.floor(table * (1.0 / BASE))
    low = table - high * BASE
    digits = jnp.concatenate([high, low, jnp.zeros((6, pages), jnp.float32)], axis=0)
    info_ref[...] = jnp.zeros_like(info_ref)
    found = []
    for q in range(queries):
        ids = candidates_ref[q : q + 1, :]
        hit = lax.broadcasted_iota(jnp.int32, (pages, cand), 0) == ids
        found.append(
            lax.dot_general(
                digits.astype(jnp.bfloat16),
                hit.astype(jnp.float32).astype(jnp.bfloat16),
                (((1,), (0,)), ((), ())),
                preferred_element_type=jnp.float32,
            )
        )
    line = jnp.concatenate(found * repeat, axis=1)
    for r in range(blocks):
        part = line[:, r * LANES : (r + 1) * LANES].astype(jnp.bfloat16)
        info_ref[r : r + 1, :] = part[0:1, :]
        info_ref[blocks + r : blocks + r + 1, :] = part[1:2, :]


def lookup(candidates, page_rows):
    return pl.pallas_call(
        lookup_kernel,
        out_shape=jax.ShapeDtypeStruct((16, LANES), jnp.bfloat16),
        in_specs=[VMEM, VMEM],
        out_specs=VMEM,
        compiler_params=pltpu.CompilerParams(vmem_limit_bytes=4 << 20),
        name="lookup",
    )(candidates, page_rows.reshape(1, -1))


def main_kernel(planes, parts, queries, cand, tokens, packed_ref, gallery_ref, out_ref, token_ref, best_ref):
    pages, patches, dim = gallery_ref.shape
    plane_rows = queries * tokens
    stride = plane_rows + 16
    count = queries * cand
    repeat = max(1, LANES // count)
    blocks = count * repeat // LANES
    held_tokens = tokens // repeat
    me = lax.axis_index("pages")
    for d in range(planes):
        token_ref[d * plane_rows : (d + 1) * plane_rows, :] = packed_ref[d * stride : d * stride + plane_rows, :]
    columns = planes * plane_rows
    step = min(columns, 256)

    def one_page(p, carry):
        patch = gallery_ref[p]
        for c in range(0, columns, step):
            sims = lax.dot_general(
                patch,
                token_ref[c : c + step, :],
                (((1,), (1,)), ((), ())),
                preferred_element_type=jnp.float32,
            )
            best_ref[pl.ds(p, 1), c : c + step] = jnp.max(sims, axis=0, keepdims=True)
        return carry

    lax.fori_loop(0, pages, one_page, 0, unroll=4 if columns == step else 1)

    lane = lax.broadcasted_iota(jnp.int32, (1, LANES), 1)
    for d in range(planes):
        dest = jnp.bitwise_xor(me, d)
        base = d * stride + plane_rows
        block = best_ref[:, d * plane_rows : (d + 1) * plane_rows]
        for r in range(blocks):
            high = packed_ref[base : base + 16, :].astype(jnp.float32)
            rows = (high[r : r + 1, :] * BASE + high[blocks + r : blocks + r + 1, :]).astype(jnp.int32)
            local = rows - me * pages
            held = (local >= 0) & (local < pages)
            pick = (lax.broadcasted_iota(jnp.int32, (pages, LANES), 0) == local).astype(jnp.float32)
            got = lax.dot_general(
                block,
                pick,
                (((0,), (0,)), ((), ())),
                precision=lax.Precision.HIGHEST,
                preferred_element_type=jnp.float32,
            )
            owner = ((r * LANES + lane) % count) // cand
            mine = got[0:tokens, :]
            for q in range(1, queries):
                mine = jnp.where(owner == q, got[q * tokens : (q + 1) * tokens, :], mine)
            mine = jnp.where(held, mine, -jnp.inf)
            line = mine[0:held_tokens, :]
            for k in range(1, repeat):
                line = jnp.where(lane // count == k, mine[k * held_tokens : (k + 1) * held_tokens, :], line)
            for j in range(parts):
                out_ref[dest * parts + j, r] = line


def finish_kernel(queries, cand, tokens, arrived_ref, scores_ref):
    count = queries * cand
    repeat = max(1, LANES // count)
    sources, blocks = arrived_ref.shape[:2]
    lines = []
    for r in range(blocks):
        best = arrived_ref[0, r]
        for s in range(1, sources):
            best = jnp.maximum(best, arrived_ref[s, r])
        total = jnp.sum(best, axis=0, keepdims=True)
        line = total[:, : LANES // repeat]
        for k in range(1, repeat):
            line = line + total[:, k * count : (k + 1) * count]
        lines.append(line)
    line = lines[0] if blocks == 1 else jnp.concatenate(lines, axis=1)
    for q in range(queries):
        scores_ref[q : q + 1, :] = line[:, q * cand : (q + 1) * cand] * (1.0 / tokens)


def body(queries, gallery, page_rows, candidates):
    planes = lax.axis_size("pages")
    parts = lax.axis_size("patches")
    everyone = planes * parts
    query_count, _, dim = queries.shape
    tokens = queries.shape[1] * parts
    cand = candidates.shape[1]
    count = query_count * cand
    repeat = max(1, LANES // count)
    blocks = count * repeat // LANES
    pages, patches, _ = gallery.shape
    here = lax.axis_index("patches")

    def swap(x, mask):
        return lax.ppermute(x, GROUP, [(i, i ^ mask) for i in range(everyone)])

    held = queries
    bit = 1
    while bit < parts:
        other = swap(held, bit if bit == 1 else bit | 1)
        upper = (here & bit) != 0
        first = jnp.where(upper, other, held)
        second = jnp.where(upper, held, other)
        held = jnp.concatenate([first, second], axis=1)
        bit *= 2
    info = lookup(candidates, page_rows)
    packed = jnp.concatenate([held.reshape(query_count * tokens, dim), info], axis=0)
    bit = 1
    while bit < planes:
        packed = jnp.concatenate([packed, swap(packed, (bit * parts) | 1)], axis=0)
        bit *= 2

    columns = planes * query_count * tokens
    message = (everyone, blocks, tokens // repeat, LANES)
    sent = pl.pallas_call(
        functools.partial(main_kernel, planes, parts, query_count, cand, tokens),
        out_shape=jax.ShapeDtypeStruct(message, jnp.float32),
        in_specs=[VMEM, VMEM],
        out_specs=VMEM,
        scratch_shapes=[
            pltpu.VMEM((columns, dim), jnp.bfloat16),
            pltpu.VMEM((pages, columns), jnp.float32),
        ],
        compiler_params=pltpu.CompilerParams(vmem_limit_bytes=40 << 20),
        name="maxima",
    )(packed, gallery)
    arrived = lax.all_to_all(sent, GROUP, split_axis=0, concat_axis=0, tiled=True)
    return pl.pallas_call(
        functools.partial(finish_kernel, query_count, cand, tokens),
        out_shape=jax.ShapeDtypeStruct((query_count, cand), jnp.float32),
        in_specs=[VMEM],
        out_specs=VMEM,
        compiler_params=pltpu.CompilerParams(vmem_limit_bytes=40 << 20),
        name="finish",
    )(arrived)


def solution(mesh):
    in_specs = (
        P(("groups", "pages"), "patches", None),
        P(("groups", "pages"), "patches", None),
        P("groups"),
        P(("groups", "pages"), None),
    )
    out_specs = P(("groups", "pages"), None)
    return jax.shard_map(body, mesh=mesh, in_specs=in_specs, out_specs=out_specs, check_vma=False)
```

```python
import functools

import jax
import jax.numpy as jnp
from jax import lax
from jax.experimental import pallas as pl
from jax.experimental.pallas import tpu as pltpu
from jax.sharding import PartitionSpec as P

LANES = 128
SUBLANES = 8
BASE = 128
INFO = 8
GROUP_PAGES = 16
LOADS = 4
GROUP = ("pages", "patches")
VMEM = pl.BlockSpec(memory_space=pltpu.VMEM)
HBM = pl.BlockSpec(memory_space=pltpu.HBM)


def sizes(queries, cand):
    count = queries * cand
    repeat = max(1, LANES // count)
    return count, repeat, count * repeat // LANES


def start_kernel(candidates_hbm, page_rows_hbm, tokens_hbm, info_ref, tokens_ref, candidates_ref, page_rows_ref, sems):
    copies = [
        pltpu.make_async_copy(page_rows_hbm, page_rows_ref, sems.at[0]),
        pltpu.make_async_copy(candidates_hbm, candidates_ref, sems.at[1]),
        pltpu.make_async_copy(tokens_hbm, tokens_ref, sems.at[2]),
    ]
    for copy in copies:
        copy.start()
    for copy in copies:
        copy.wait()
    queries, cand = candidates_ref.shape
    pages = page_rows_ref.shape[0]
    _, repeat, blocks = sizes(queries, cand)
    table = page_rows_ref[...].reshape(1, pages).astype(jnp.float32)
    high = jnp.floor(table * (1.0 / BASE))
    low = table - high * BASE
    digits = jnp.concatenate([high, low, jnp.zeros((6, pages), jnp.float32)], axis=0)
    found = []
    for q in range(queries):
        ids = candidates_ref[q : q + 1, :]
        hit = lax.broadcasted_iota(jnp.int32, (pages, cand), 0) == ids
        found.append(
            lax.dot_general(
                digits.astype(jnp.bfloat16),
                hit.astype(jnp.float32).astype(jnp.bfloat16),
                (((1,), (0,)), ((), ())),
                preferred_element_type=jnp.float32,
            )
        )
    line = jnp.concatenate(found * repeat, axis=1)
    rows = [line[0:1, r * LANES : (r + 1) * LANES] for r in range(blocks)]
    rows += [line[1:2, r * LANES : (r + 1) * LANES] for r in range(blocks)]
    if 2 * blocks < INFO:
        rows.append(jnp.zeros((INFO - 2 * blocks, LANES), jnp.float32))
    info_ref[...] = jnp.concatenate(rows, axis=0).astype(jnp.bfloat16)


def in_hbm(x):
    return pltpu.with_memory_space_constraint(x, pltpu.HBM)


def start(candidates, page_rows, tokens):
    return pl.pallas_call(
        start_kernel,
        out_shape=(jax.ShapeDtypeStruct((INFO, LANES), jnp.bfloat16), jax.ShapeDtypeStruct(tokens.shape, tokens.dtype)),
        in_specs=[HBM, HBM, HBM],
        out_specs=(VMEM, VMEM),
        scratch_shapes=[
            pltpu.VMEM(candidates.shape, jnp.int32),
            pltpu.VMEM(page_rows.shape, jnp.int32),
            pltpu.SemaphoreType.DMA((3,)),
        ],
        compiler_params=pltpu.CompilerParams(vmem_limit_bytes=8 << 20),
        cost_estimate=pl.CostEstimate(flops=1 << 20, transcendentals=0, bytes_accessed=1 << 20),
        name="start",
    )(in_hbm(candidates), in_hbm(page_rows), in_hbm(tokens))


def load_kernel(first, gallery_hbm, out_ref, sems):
    share = out_ref.shape[0] // LOADS
    copies = [
        pltpu.make_async_copy(
            gallery_hbm.at[pl.ds(first + i * share, share)], out_ref.at[pl.ds(i * share, share)], sems.at[i]
        )
        for i in range(LOADS)
    ]
    for copy in copies:
        copy.start()
    for copy in copies:
        copy.wait()


def load(gallery, first, count):
    shape = (count, *gallery.shape[1:])
    return pl.pallas_call(
        functools.partial(load_kernel, first),
        out_shape=jax.ShapeDtypeStruct(shape, gallery.dtype),
        in_specs=[HBM],
        out_specs=VMEM,
        scratch_shapes=[pltpu.SemaphoreType.DMA((LOADS,))],
        cost_estimate=pl.CostEstimate(
            flops=0, transcendentals=0, bytes_accessed=4 * count * gallery.shape[1] * gallery.shape[2]
        ),
        compiler_params=pltpu.CompilerParams(vmem_limit_bytes=8 << 20),
        name="load",
    )(in_hbm(gallery))


def main_kernel(queries, cand, order, shift, packed_ref, *refs):
    *gallery_refs, out_ref, token_ref, best_ref = refs
    patches, dim = gallery_refs[0].shape[1:]
    pages = best_ref.shape[0]
    columns = token_ref.shape[0]
    pieces = len(order[0])
    planes = len(order)
    plane_rows = columns // planes
    piece_rows = plane_rows // pieces
    unit = plane_rows + INFO
    each = piece_rows // queries
    tokens = each * pieces
    count, repeat, blocks = sizes(queries, cand)
    held_tokens = tokens // repeat
    here = lax.shift_right_logical(lax.axis_index("patches"), shift)
    for d in range(planes):
        for i, flip in enumerate(order[d]):
            at = d * plane_rows + jnp.bitwise_xor(here, flip) * piece_rows
            start = d * unit + i * piece_rows
            token_ref[pl.ds(pl.multiple_of(at, piece_rows), piece_rows), :] = packed_ref[start : start + piece_rows, :]

    width = min(columns, 256)

    def some_pages(gallery_ref, begin, i, carry):
        at = pl.multiple_of(i * GROUP_PAGES, GROUP_PAGES)
        patch = gallery_ref[pl.ds(at, GROUP_PAGES)].reshape(GROUP_PAGES * patches, dim)
        for c in range(0, columns, width):
            sims = lax.dot_general(
                patch,
                token_ref[c : c + width, :],
                (((1,), (1,)), ((), ())),
                preferred_element_type=jnp.float32,
            )
            best_ref[pl.ds(begin + at, GROUP_PAGES), c : c + width] = jnp.max(
                sims.reshape(GROUP_PAGES, patches, width), axis=1
            )
        return carry

    begin = 0
    for ref in gallery_refs:
        lax.fori_loop(0, ref.shape[0] // GROUP_PAGES, functools.partial(some_pages, ref, begin), 0)
        begin += ref.shape[0]

    first = lax.axis_index("pages") * pages
    lane = lax.broadcasted_iota(jnp.int32, (1, LANES), 1)
    for d in range(planes):
        block = best_ref[:, d * plane_rows : (d + 1) * plane_rows]
        info = packed_ref[d * unit + plane_rows : (d + 1) * unit, :].astype(jnp.float32)
        for r in range(blocks):
            rows = (info[r : r + 1, :] * BASE + info[blocks + r : blocks + r + 1, :]).astype(jnp.int32)
            local = rows - first
            held = (local >= 0) & (local < pages)
            pick = (lax.broadcasted_iota(jnp.int32, (pages, LANES), 0) == local).astype(jnp.float32)
            got = lax.dot_general(
                block,
                pick,
                (((0,), (0,)), ((), ())),
                precision=lax.Precision.HIGHEST,
                preferred_element_type=jnp.float32,
            )
            owner = ((r * LANES + lane) % count) // cand
            parts = []
            for i in range(pieces):
                at = i * piece_rows
                mine = got[at : at + each, :]
                for q in range(1, queries):
                    mine = jnp.where(owner == q, got[at + q * each : at + (q + 1) * each, :], mine)
                parts.append(mine)
            mine = jnp.where(held, jnp.concatenate(parts, axis=0), -jnp.inf)
            line = mine[0:held_tokens, :]
            for k in range(1, repeat):
                line = jnp.where(lane // count == k, mine[k * held_tokens : (k + 1) * held_tokens, :], line)
            out_ref[d, r] = line


def finish_kernel(queries, cand, tokens, mine_ref, other_ref, scores_ref):
    count, repeat, blocks = sizes(queries, cand)
    lines = []
    for r in range(blocks):
        best = jnp.maximum(mine_ref[r], other_ref[r])
        total = jnp.sum(best, axis=0, keepdims=True)
        line = total[:, : LANES // repeat]
        for k in range(1, repeat):
            line = line + total[:, k * count : (k + 1) * count]
        lines.append(line)
    line = lines[0] if blocks == 1 else jnp.concatenate(lines, axis=1)
    for q in range(queries):
        scores_ref[q : q + 1, :] = line[:, q * cand : (q + 1) * cand] * (1.0 / tokens)


def body(queries, gallery, page_rows, candidates):
    planes = lax.axis_size("pages")
    parts = lax.axis_size("patches")
    everyone = planes * parts
    query_count, own_tokens, dim = queries.shape
    tokens = own_tokens * parts
    cand = candidates.shape[1]
    _, repeat, blocks = sizes(query_count, cand)
    pages, patches, _ = gallery.shape

    def swap(x, mask):
        return lax.ppermute(x, GROUP, [(i, i ^ mask) for i in range(everyone)])

    def mask_of(bit):
        return bit if bit == 1 else bit | 1

    info, own = start(candidates, page_rows, queries)
    parts_of_gallery = [load(gallery, 0, 32), load(gallery, 32, 48)]
    held, bit, shift = queries, 1, 0
    while held.shape[1] % SUBLANES and bit < parts:
        other = swap(held, mask_of(bit))
        upper = (lax.axis_index("patches") & bit) != 0
        held = jnp.concatenate([jnp.where(upper, other, held), jnp.where(upper, held, other)], axis=1)
        bit, shift = bit * 2, shift + 1
    packed = held.reshape(-1, dim)
    order = [0]
    while bit < parts:
        mask = mask_of(bit)
        packed = jnp.concatenate([own.reshape(packed.shape) if bit == 1 else packed, swap(packed, mask)], axis=0)
        order = order + [(mask >> shift) ^ flip for flip in order]
        bit *= 2
    packed = jnp.concatenate([packed, info], axis=0)
    order = [order]
    bit = 1
    while bit < planes:
        mask = (bit * parts) | 1
        packed = jnp.concatenate([packed, swap(packed, mask)], axis=0)
        order = order + [[((mask % parts) >> shift) ^ flip for flip in flips] for flips in order]
        bit *= 2

    columns = planes * query_count * tokens
    best = pl.pallas_call(
        functools.partial(main_kernel, query_count, cand, order, shift),
        out_shape=jax.ShapeDtypeStruct((planes, blocks, tokens // repeat, LANES), jnp.float32),
        in_specs=[VMEM] * (1 + len(parts_of_gallery)),
        out_specs=VMEM,
        scratch_shapes=[
            pltpu.VMEM((columns, dim), jnp.bfloat16),
            pltpu.VMEM((pages, columns), jnp.float32),
        ],
        compiler_params=pltpu.CompilerParams(vmem_limit_bytes=24 << 20),
        name="maxima",
    )(packed, *parts_of_gallery)
    while bit > 1:
        bit //= 2
        best = jnp.maximum(best[:bit], swap(best[bit:], (bit * parts) | 1))
    best = best[0]
    bit = parts // 2
    while bit > 1:
        best = jnp.maximum(best, swap(best, mask_of(bit)))
        bit //= 2
    return pl.pallas_call(
        functools.partial(finish_kernel, query_count, cand, tokens),
        out_shape=jax.ShapeDtypeStruct((query_count, cand), jnp.float32),
        in_specs=[VMEM, VMEM],
        out_specs=VMEM,
        compiler_params=pltpu.CompilerParams(vmem_limit_bytes=8 << 20),
        name="finish",
    )(best, swap(best, 1))


def solution(mesh):
    in_specs = (
        P(("groups", "pages"), "patches", None),
        P(("groups", "pages"), "patches", None),
        P("groups"),
        P(("groups", "pages"), None),
    )
    out_specs = P(("groups", "pages"), None)
    return jax.shard_map(body, mesh=mesh, in_specs=in_specs, out_specs=out_specs, check_vma=False)
```

```python
import functools

import jax
import jax.numpy as jnp
from jax import lax
from jax.experimental import pallas as pl
from jax.experimental.pallas import tpu as pltpu
from jax.sharding import PartitionSpec as P

LANES = 128
SUBLANES = 8
BASE = 128
INFO = 8
GROUP_PAGES = 16
LOADS = 4
LOAD_PAGES = 32
GROUP = ("pages", "patches")
VMEM = pl.BlockSpec(memory_space=pltpu.VMEM)
HBM = pl.BlockSpec(memory_space=pltpu.HBM)


def sizes(queries, cand):
    count = queries * cand
    repeat = max(1, LANES // count)
    return count, repeat, count * repeat // LANES


def start_kernel(candidates_hbm, page_rows_hbm, tokens_hbm, info_ref, tokens_ref, candidates_ref, page_rows_ref, sems):
    copies = [
        pltpu.make_async_copy(page_rows_hbm, page_rows_ref, sems.at[0]),
        pltpu.make_async_copy(candidates_hbm, candidates_ref, sems.at[1]),
        pltpu.make_async_copy(tokens_hbm, tokens_ref, sems.at[2]),
    ]
    for copy in copies:
        copy.start()
    for copy in copies:
        copy.wait()
    queries, cand = candidates_ref.shape
    pages = page_rows_ref.shape[0]
    _, repeat, blocks = sizes(queries, cand)
    table = page_rows_ref[...].reshape(1, pages).astype(jnp.float32)
    high = jnp.floor(table * (1.0 / BASE))
    low = table - high * BASE
    digits = jnp.concatenate([high, low, jnp.zeros((6, pages), jnp.float32)], axis=0)
    found = []
    for q in range(queries):
        ids = candidates_ref[q : q + 1, :]
        hit = lax.broadcasted_iota(jnp.int32, (pages, cand), 0) == ids
        found.append(
            lax.dot_general(
                digits.astype(jnp.bfloat16),
                hit.astype(jnp.float32).astype(jnp.bfloat16),
                (((1,), (0,)), ((), ())),
                preferred_element_type=jnp.float32,
            )
        )
    line = jnp.concatenate(found * repeat, axis=1)
    rows = [line[0:1, r * LANES : (r + 1) * LANES] for r in range(blocks)]
    rows += [line[1:2, r * LANES : (r + 1) * LANES] for r in range(blocks)]
    if 2 * blocks < INFO:
        rows.append(jnp.zeros((INFO - 2 * blocks, LANES), jnp.float32))
    info_ref[...] = jnp.concatenate(rows, axis=0).astype(jnp.bfloat16)


def in_hbm(x):
    return pltpu.with_memory_space_constraint(x, pltpu.HBM)


def start(candidates, page_rows, tokens):
    return pl.pallas_call(
        start_kernel,
        out_shape=(jax.ShapeDtypeStruct((INFO, LANES), jnp.bfloat16), jax.ShapeDtypeStruct(tokens.shape, tokens.dtype)),
        in_specs=[HBM, HBM, HBM],
        out_specs=(VMEM, VMEM),
        scratch_shapes=[
            pltpu.VMEM(candidates.shape, jnp.int32),
            pltpu.VMEM(page_rows.shape, jnp.int32),
            pltpu.SemaphoreType.DMA((3,)),
        ],
        compiler_params=pltpu.CompilerParams(vmem_limit_bytes=8 << 20),
        cost_estimate=pl.CostEstimate(flops=1 << 20, transcendentals=0, bytes_accessed=1 << 20),
        name="start",
    )(in_hbm(candidates), in_hbm(page_rows), in_hbm(tokens))


def load_kernel(first, gallery_hbm, out_ref, sems):
    share = out_ref.shape[0] // LOADS
    copies = [
        pltpu.make_async_copy(
            gallery_hbm.at[pl.ds(first + i * share, share)], out_ref.at[pl.ds(i * share, share)], sems.at[i]
        )
        for i in range(LOADS)
    ]
    for copy in copies:
        copy.start()
    for copy in copies:
        copy.wait()


def load(gallery, first, count):
    shape = (count, *gallery.shape[1:])
    return pl.pallas_call(
        functools.partial(load_kernel, first),
        out_shape=jax.ShapeDtypeStruct(shape, gallery.dtype),
        in_specs=[HBM],
        out_specs=VMEM,
        scratch_shapes=[pltpu.SemaphoreType.DMA((LOADS,))],
        cost_estimate=pl.CostEstimate(
            flops=0, transcendentals=0, bytes_accessed=4 * count * gallery.shape[1] * gallery.shape[2]
        ),
        compiler_params=pltpu.CompilerParams(vmem_limit_bytes=8 << 20),
    )(in_hbm(gallery))


def main_kernel(queries, cand, order, shift, loaded, packed_ref, *refs):
    *held_refs, gallery_hbm, out_ref, token_ref, best_ref, rest_ref, sems = refs
    pages, patches, dim = gallery_hbm.shape
    steps = rest_ref.shape[0] // GROUP_PAGES

    def fetch(i):
        source = gallery_hbm.at[pl.ds(loaded + i * GROUP_PAGES, GROUP_PAGES)]
        return pltpu.make_async_copy(source, rest_ref.at[pl.ds(i * GROUP_PAGES, GROUP_PAGES)], sems.at[i])

    for i in range(steps):
        fetch(i).start()
    pieces = len(order[0])
    planes = len(order)
    columns = best_ref.shape[1]
    plane_rows = columns // planes
    piece_rows = plane_rows // pieces
    unit = plane_rows + INFO
    each = piece_rows // queries
    tokens = each * pieces
    count, repeat, blocks = sizes(queries, cand)
    held_tokens = tokens // repeat
    here = lax.shift_right_logical(lax.axis_index("patches"), shift)
    double = token_ref.shape[1] // dim
    if double == 2:
        token_ref[...] = jnp.zeros_like(token_ref)
    for d in range(planes):
        for i, flip in enumerate(order[d]):
            at = d * plane_rows + jnp.bitwise_xor(here, flip) * piece_rows
            start = d * unit + i * piece_rows
            piece = packed_ref[start : start + piece_rows, :]
            for k in range(double):
                rows = pl.ds(pl.multiple_of(at + k * columns, piece_rows), piece_rows)
                token_ref[rows, k * dim : (k + 1) * dim] = piece

    width = min(columns, 256)

    def some_pages(gallery_ref, begin, i):
        at = pl.multiple_of(i * GROUP_PAGES, GROUP_PAGES)
        share = GROUP_PAGES // double
        sides = [gallery_ref[pl.ds(at + k * share, share)].reshape(share * patches, dim) for k in range(double)]
        patch = sides[0] if double == 1 else jnp.concatenate(sides, axis=1)
        for c in range(0, columns, width):
            sims = lax.dot_general(
                patch,
                token_ref[c : c + width * double, :],
                (((1,), (1,)), ((), ())),
                preferred_element_type=jnp.float32,
            )
            top = jnp.max(sims.reshape(share, patches, width * double), axis=1)
            for k in range(double):
                best_ref[pl.ds(begin + at + k * share, share), c : c + width] = top[:, k * width : (k + 1) * width]

    def run(ref, begin, i, carry):
        some_pages(ref, begin, i)
        return carry

    def run_rest(i, carry):
        fetch(i).wait()
        some_pages(rest_ref, loaded, i)
        return carry

    begin = 0
    for ref in held_refs:
        lax.fori_loop(0, ref.shape[0] // GROUP_PAGES, functools.partial(run, ref, begin), 0)
        begin += ref.shape[0]
    lax.fori_loop(0, steps, run_rest, 0)

    first = lax.axis_index("pages") * pages
    lane = lax.broadcasted_iota(jnp.int32, (1, LANES), 1)
    for d in range(planes):
        block = best_ref[:, d * plane_rows : (d + 1) * plane_rows]
        info = packed_ref[d * unit + plane_rows : (d + 1) * unit, :].astype(jnp.float32)
        for r in range(blocks):
            rows = (info[r : r + 1, :] * BASE + info[blocks + r : blocks + r + 1, :]).astype(jnp.int32)
            local = rows - first
            held = (local >= 0) & (local < pages)
            pick = (lax.broadcasted_iota(jnp.int32, (pages, LANES), 0) == local).astype(jnp.float32)
            got = lax.dot_general(
                block,
                pick,
                (((0,), (0,)), ((), ())),
                precision=lax.Precision.HIGHEST,
                preferred_element_type=jnp.float32,
            )
            owner = ((r * LANES + lane) % count) // cand
            parts = []
            for i in range(pieces):
                at = i * piece_rows
                mine = got[at : at + each, :]
                for q in range(1, queries):
                    mine = jnp.where(owner == q, got[at + q * each : at + (q + 1) * each, :], mine)
                parts.append(mine)
            mine = jnp.where(held, jnp.concatenate(parts, axis=0), -jnp.inf)
            line = mine[0:held_tokens, :]
            for k in range(1, repeat):
                line = jnp.where(lane // count == k, mine[k * held_tokens : (k + 1) * held_tokens, :], line)
            out_ref[d, r] = line


def finish_kernel(queries, cand, tokens, mine_ref, other_ref, scores_ref):
    count, repeat, blocks = sizes(queries, cand)
    lines = []
    for r in range(blocks):
        best = jnp.maximum(mine_ref[r], other_ref[r])
        total = jnp.sum(best, axis=0, keepdims=True)
        line = total[:, : LANES // repeat]
        for k in range(1, repeat):
            line = line + total[:, k * count : (k + 1) * count]
        lines.append(line)
    line = lines[0] if blocks == 1 else jnp.concatenate(lines, axis=1)
    for q in range(queries):
        scores_ref[q : q + 1, :] = line[:, q * cand : (q + 1) * cand] * (1.0 / tokens)


def body(queries, gallery, page_rows, candidates):
    planes = lax.axis_size("pages")
    parts = lax.axis_size("patches")
    everyone = planes * parts
    query_count, own_tokens, dim = queries.shape
    tokens = own_tokens * parts
    cand = candidates.shape[1]
    _, repeat, blocks = sizes(query_count, cand)
    pages, patches, _ = gallery.shape

    def swap(x, mask):
        return lax.ppermute(x, GROUP, [(i, i ^ mask) for i in range(everyone)])

    def mask_of(bit):
        return bit if bit == 1 else bit | 1

    info, own = start(candidates, page_rows, queries)
    loaded = [load(gallery, 0, LOAD_PAGES), load(gallery, LOAD_PAGES, LOAD_PAGES)]
    held, bit, shift = queries, 1, 0
    while held.shape[1] % SUBLANES and bit < parts:
        other = swap(held, mask_of(bit))
        upper = (lax.axis_index("patches") & bit) != 0
        held = jnp.concatenate([jnp.where(upper, other, held), jnp.where(upper, held, other)], axis=1)
        bit, shift = bit * 2, shift + 1
    packed = held.reshape(-1, dim)
    order = [0]
    while bit < parts:
        mask = mask_of(bit)
        other = swap(packed, mask)
        packed = jnp.concatenate([own.reshape(packed.shape) if bit == 1 else packed, other], axis=0)
        order = order + [(mask >> shift) ^ flip for flip in order]
        bit *= 2
    packed = jnp.concatenate([packed, info], axis=0)
    order = [order]

    def maxima(packed, order):
        columns = len(order) * query_count * tokens
        double = 2 if columns <= 128 else 1
        rest = pages - 2 * LOAD_PAGES
        return pl.pallas_call(
            functools.partial(main_kernel, query_count, cand, order, shift, 2 * LOAD_PAGES),
            out_shape=jax.ShapeDtypeStruct((len(order), blocks, tokens // repeat, LANES), jnp.float32),
            in_specs=[VMEM, VMEM, VMEM, HBM],
            out_specs=VMEM,
            scratch_shapes=[
                pltpu.VMEM((columns * double, dim * double), jnp.bfloat16),
                pltpu.VMEM((pages, columns), jnp.float32),
                pltpu.VMEM((rest, patches, dim), jnp.bfloat16),
                pltpu.SemaphoreType.DMA((rest // GROUP_PAGES,)),
            ],
            cost_estimate=pl.CostEstimate(
                flops=2 * pages * patches * dim * columns, transcendentals=0, bytes_accessed=2 * gallery.size
            ),
            compiler_params=pltpu.CompilerParams(vmem_limit_bytes=24 << 20),
        )(packed, *loaded, in_hbm(gallery))

    bit = 1
    while bit < planes:
        mask = (bit * parts) | 1
        last = bit == planes // 2
        other = swap(packed, mask)
        flips = [[((mask % parts) >> shift) ^ flip for flip in flips] for flips in order]
        if last:
            near = maxima(packed, order)
            far = maxima(other, flips)
        else:
            packed = jnp.concatenate([packed, other], axis=0)
            order = order + flips
        bit *= 2

    while bit > 1:
        bit //= 2
        arrived = swap(far, (bit * parts) | 1)
        best = jnp.maximum(near, arrived)
        near, far = best[: bit // 2], best[bit // 2 :]
    best = best[0]
    bit = parts // 2
    while bit > 1:
        best = jnp.maximum(best, swap(best, mask_of(bit)))
        bit //= 2
    return pl.pallas_call(
        functools.partial(finish_kernel, query_count, cand, tokens),
        out_shape=jax.ShapeDtypeStruct((query_count, cand), jnp.float32),
        in_specs=[VMEM, VMEM],
        out_specs=VMEM,
        compiler_params=pltpu.CompilerParams(vmem_limit_bytes=8 << 20),
        name="finish",
    )(best, swap(best, 1))


def solution(mesh):
    in_specs = (
        P(("groups", "pages"), "patches", None),
        P(("groups", "pages"), "patches", None),
        P("groups"),
        P(("groups", "pages"), None),
    )
    out_specs = P(("groups", "pages"), None)
    return jax.shard_map(body, mesh=mesh, in_specs=in_specs, out_specs=out_specs, check_vma=False)
```

```python
import functools

import jax
import jax.numpy as jnp
from jax import lax
from jax.experimental import pallas as pl
from jax.experimental.pallas import tpu as pltpu
from jax.sharding import PartitionSpec as P

LANES = 128
SUBLANES = 8
BASE = 128
INFO = 8
GROUP_PAGES = 16
LOADS = 4
GROUP = ("pages", "patches")
VMEM = pl.BlockSpec(memory_space=pltpu.VMEM)
HBM = pl.BlockSpec(memory_space=pltpu.HBM)


def sizes(queries, cand):
    count = queries * cand
    repeat = max(1, LANES // count)
    return count, repeat, count * repeat // LANES


def start_kernel(candidates_hbm, page_rows_hbm, tokens_hbm, info_ref, tokens_ref, candidates_ref, page_rows_ref, sems):
    copies = [
        pltpu.make_async_copy(page_rows_hbm, page_rows_ref, sems.at[0]),
        pltpu.make_async_copy(candidates_hbm, candidates_ref, sems.at[1]),
        pltpu.make_async_copy(tokens_hbm, tokens_ref, sems.at[2]),
    ]
    for copy in copies:
        copy.start()
    for copy in copies:
        copy.wait()
    queries, cand = candidates_ref.shape
    pages = page_rows_ref.shape[0]
    _, repeat, blocks = sizes(queries, cand)
    table = page_rows_ref[...].reshape(1, pages).astype(jnp.float32)
    high = jnp.floor(table * (1.0 / BASE))
    low = table - high * BASE
    digits = jnp.concatenate([high, low, jnp.zeros((6, pages), jnp.float32)], axis=0)
    found = []
    for q in range(queries):
        ids = candidates_ref[q : q + 1, :]
        hit = lax.broadcasted_iota(jnp.int32, (pages, cand), 0) == ids
        found.append(
            lax.dot_general(
                digits.astype(jnp.bfloat16),
                hit.astype(jnp.float32).astype(jnp.bfloat16),
                (((1,), (0,)), ((), ())),
                preferred_element_type=jnp.float32,
            )
        )
    line = jnp.concatenate(found * repeat, axis=1)
    rows = [line[0:1, r * LANES : (r + 1) * LANES] for r in range(blocks)]
    rows += [line[1:2, r * LANES : (r + 1) * LANES] for r in range(blocks)]
    if 2 * blocks < INFO:
        rows.append(jnp.zeros((INFO - 2 * blocks, LANES), jnp.float32))
    info_ref[...] = jnp.concatenate(rows, axis=0).astype(jnp.bfloat16)


def in_hbm(x):
    return pltpu.with_memory_space_constraint(x, pltpu.HBM)


def start(candidates, page_rows, tokens):
    return pl.pallas_call(
        start_kernel,
        out_shape=(jax.ShapeDtypeStruct((INFO, LANES), jnp.bfloat16), jax.ShapeDtypeStruct(tokens.shape, tokens.dtype)),
        in_specs=[HBM, HBM, HBM],
        out_specs=(VMEM, VMEM),
        scratch_shapes=[
            pltpu.VMEM(candidates.shape, jnp.int32),
            pltpu.VMEM(page_rows.shape, jnp.int32),
            pltpu.SemaphoreType.DMA((3,)),
        ],
        compiler_params=pltpu.CompilerParams(vmem_limit_bytes=8 << 20),
        cost_estimate=pl.CostEstimate(flops=1 << 20, transcendentals=0, bytes_accessed=1 << 20),
        name="start",
    )(in_hbm(candidates), in_hbm(page_rows), in_hbm(tokens))


def load_kernel(first, gallery_hbm, out_ref, sems):
    share = out_ref.shape[0] // LOADS
    copies = [
        pltpu.make_async_copy(
            gallery_hbm.at[pl.ds(first + i * share, share)], out_ref.at[pl.ds(i * share, share)], sems.at[i]
        )
        for i in range(LOADS)
    ]
    for copy in copies:
        copy.start()
    for copy in copies:
        copy.wait()


def load(gallery, first, count):
    shape = (count, *gallery.shape[1:])
    return pl.pallas_call(
        functools.partial(load_kernel, first),
        out_shape=jax.ShapeDtypeStruct(shape, gallery.dtype),
        in_specs=[HBM],
        out_specs=VMEM,
        scratch_shapes=[pltpu.SemaphoreType.DMA((LOADS,))],
        cost_estimate=pl.CostEstimate(
            flops=0, transcendentals=0, bytes_accessed=4 * count * gallery.shape[1] * gallery.shape[2]
        ),
        compiler_params=pltpu.CompilerParams(vmem_limit_bytes=8 << 20),
    )(in_hbm(gallery))


def shapes(order, columns, queries):
    plane_rows = columns // len(order)
    piece_rows = plane_rows // len(order[0])
    return plane_rows, piece_rows, piece_rows // queries


def arrange(order, columns, queries, shift, packed_ref, token_ref):
    plane_rows, piece_rows, _ = shapes(order, columns, queries)
    dim = packed_ref.shape[1]
    unit = plane_rows + INFO
    here = lax.shift_right_logical(lax.axis_index("patches"), shift)
    double = token_ref.shape[1] // dim
    if double == 2:
        token_ref[...] = jnp.zeros_like(token_ref)
    for d in range(len(order)):
        for i, flip in enumerate(order[d]):
            at = d * plane_rows + jnp.bitwise_xor(here, flip) * piece_rows
            start = d * unit + i * piece_rows
            piece = packed_ref[start : start + piece_rows, :]
            for k in range(double):
                rows = pl.ds(pl.multiple_of(at + k * columns, piece_rows), piece_rows)
                token_ref[rows, k * dim : (k + 1) * dim] = piece


def scan(gallery_ref, begin, token_ref, best_ref):
    pages, patches, dim = gallery_ref.shape
    columns = best_ref.shape[1]
    double = token_ref.shape[1] // dim
    width = min(columns, 256)
    share = GROUP_PAGES // double

    def step(i, carry):
        at = pl.multiple_of(i * GROUP_PAGES, GROUP_PAGES)
        sides = [gallery_ref[pl.ds(at + k * share, share)].reshape(share * patches, dim) for k in range(double)]
        patch = sides[0] if double == 1 else jnp.concatenate(sides, axis=1)
        for c in range(0, columns, width):
            sims = lax.dot_general(
                patch,
                token_ref[c : c + width * double, :],
                (((1,), (1,)), ((), ())),
                preferred_element_type=jnp.float32,
            )
            top = jnp.max(sims.reshape(share, patches, width * double), axis=1)
            for k in range(double):
                best_ref[pl.ds(begin + at + k * share, share), c : c + width] = top[:, k * width : (k + 1) * width]
        return carry

    lax.fori_loop(0, pages // GROUP_PAGES, step, 0)


def select(order, queries, cand, packed_ref, best_ref, out_ref):
    pages, columns = best_ref.shape
    plane_rows, piece_rows, each = shapes(order, columns, queries)
    pieces = len(order[0])
    unit = plane_rows + INFO
    count, repeat, blocks = sizes(queries, cand)
    held_tokens = each * pieces // repeat
    first = lax.axis_index("pages") * pages
    lane = lax.broadcasted_iota(jnp.int32, (1, LANES), 1)
    for d in range(len(order)):
        block = best_ref[:, d * plane_rows : (d + 1) * plane_rows]
        info = packed_ref[d * unit + plane_rows : (d + 1) * unit, :].astype(jnp.float32)
        for r in range(blocks):
            rows = (info[r : r + 1, :] * BASE + info[blocks + r : blocks + r + 1, :]).astype(jnp.int32)
            local = rows - first
            held = (local >= 0) & (local < pages)
            pick = (lax.broadcasted_iota(jnp.int32, (pages, LANES), 0) == local).astype(jnp.float32)
            got = lax.dot_general(
                block,
                pick,
                (((0,), (0,)), ((), ())),
                precision=lax.Precision.HIGHEST,
                preferred_element_type=jnp.float32,
            )
            owner = ((r * LANES + lane) % count) // cand
            parts = []
            for i in range(pieces):
                at = i * piece_rows
                mine = got[at : at + each, :]
                for q in range(1, queries):
                    mine = jnp.where(owner == q, got[at + q * each : at + (q + 1) * each, :], mine)
                parts.append(mine)
            mine = jnp.where(held, jnp.concatenate(parts, axis=0), -jnp.inf)
            line = mine[0:held_tokens, :]
            for k in range(1, repeat):
                line = jnp.where(lane // count == k, mine[k * held_tokens : (k + 1) * held_tokens, :], line)
            out_ref[d, r] = line


def near_first_kernel(queries, order, shift, packed_ref, gallery_ref, gallery_hbm, best_ref, rest_ref, token_ref, sem):
    pages = gallery_hbm.shape[0]
    rest = rest_ref.shape[0]
    copy = pltpu.make_async_copy(gallery_hbm.at[pl.ds(pages - rest, rest)], rest_ref, sem)
    copy.start()
    arrange(order, best_ref.shape[1], queries, shift, packed_ref, token_ref)
    scan(gallery_ref, 0, token_ref, best_ref)
    copy.wait()


def near_second_kernel(queries, cand, order, shift, packed_ref, first_ref, *refs):
    *gallery_refs, out_ref, token_ref, best_ref = refs
    arrange(order, best_ref.shape[1], queries, shift, packed_ref, token_ref)
    begin = first_ref.shape[0]
    best_ref[0:begin, :] = first_ref[...]
    for ref in gallery_refs:
        scan(ref, begin, token_ref, best_ref)
        begin += ref.shape[0]
    select(order, queries, cand, packed_ref, best_ref, out_ref)


def far_kernel(queries, cand, order, shift, packed_ref, *refs):
    *gallery_refs, out_ref, token_ref, best_ref = refs
    arrange(order, best_ref.shape[1], queries, shift, packed_ref, token_ref)
    begin = 0
    for ref in gallery_refs:
        scan(ref, begin, token_ref, best_ref)
        begin += ref.shape[0]
    select(order, queries, cand, packed_ref, best_ref, out_ref)


def finish_kernel(queries, cand, tokens, mine_ref, other_ref, scores_ref):
    count, repeat, blocks = sizes(queries, cand)
    lines = []
    for r in range(blocks):
        best = jnp.maximum(mine_ref[r], other_ref[r])
        total = jnp.sum(best, axis=0, keepdims=True)
        line = total[:, : LANES // repeat]
        for k in range(1, repeat):
            line = line + total[:, k * count : (k + 1) * count]
        lines.append(line)
    line = lines[0] if blocks == 1 else jnp.concatenate(lines, axis=1)
    for q in range(queries):
        scores_ref[q : q + 1, :] = line[:, q * cand : (q + 1) * cand] * (1.0 / tokens)


def body(queries, gallery, page_rows, candidates):
    planes = lax.axis_size("pages")
    parts = lax.axis_size("patches")
    everyone = planes * parts
    query_count, own_tokens, dim = queries.shape
    tokens = own_tokens * parts
    cand = candidates.shape[1]
    _, repeat, blocks = sizes(query_count, cand)
    pages, patches, _ = gallery.shape

    def swap(x, mask):
        return lax.ppermute(x, GROUP, [(i, i ^ mask) for i in range(everyone)])

    def mask_of(bit):
        return bit if bit == 1 else bit | 1

    info, own = start(candidates, page_rows, queries)
    rest = GROUP_PAGES * max(1, pages // GROUP_PAGES // 5)
    most = pages - 2 * rest
    gallery_a = load(gallery, 0, most)
    gallery_b = load(gallery, most, rest)
    held, bit, shift = queries, 1, 0
    while held.shape[1] % SUBLANES and bit < parts:
        other = swap(held, mask_of(bit))
        upper = (lax.axis_index("patches") & bit) != 0
        held = jnp.concatenate([jnp.where(upper, other, held), jnp.where(upper, held, other)], axis=1)
        bit, shift = bit * 2, shift + 1
    packed = held.reshape(-1, dim)
    order = [0]
    while bit < parts:
        mask = mask_of(bit)
        other = swap(packed, mask)
        packed = jnp.concatenate([own.reshape(packed.shape) if bit == 1 else packed, other], axis=0)
        order = order + [(mask >> shift) ^ flip for flip in order]
        bit *= 2
    packed = jnp.concatenate([packed, info], axis=0)
    order = [order]

    columns = planes // 2 * query_count * tokens
    double = 2 if columns <= 128 else 1
    token_scratch = pltpu.VMEM((columns * double, dim * double), jnp.bfloat16)
    best_scratch = pltpu.VMEM((pages, columns), jnp.float32)
    message = jax.ShapeDtypeStruct((planes // 2, blocks, tokens // repeat, LANES), jnp.float32)

    def call(kernel, count, **kwargs):
        return pl.pallas_call(
            kernel,
            cost_estimate=pl.CostEstimate(
                flops=2 * count * patches * dim * columns, transcendentals=0, bytes_accessed=count * patches * dim * 2
            ),
            compiler_params=pltpu.CompilerParams(vmem_limit_bytes=24 << 20),
            **kwargs,
        )

    bit = 1
    while bit < planes:
        mask = (bit * parts) | 1
        last = bit == planes // 2
        other = swap(packed, mask)
        flips = [[((mask % parts) >> shift) ^ flip for flip in flips] for flips in order]
        if last:
            near_best, gallery_c = call(
                functools.partial(near_first_kernel, query_count, order, shift),
                most,
                out_shape=(
                    jax.ShapeDtypeStruct((most, columns), jnp.float32),
                    jax.ShapeDtypeStruct((rest, patches, dim), gallery.dtype),
                ),
                in_specs=[VMEM, VMEM, HBM],
                out_specs=(VMEM, VMEM),
                scratch_shapes=[token_scratch, pltpu.SemaphoreType.DMA],
            )(packed, gallery_a, in_hbm(gallery))
            far = call(
                functools.partial(far_kernel, query_count, cand, flips, shift),
                pages,
                out_shape=message,
                in_specs=[VMEM] * 4,
                out_specs=VMEM,
                scratch_shapes=[token_scratch, best_scratch],
            )(other, gallery_a, gallery_b, gallery_c)
            near = call(
                functools.partial(near_second_kernel, query_count, cand, order, shift),
                2 * rest,
                out_shape=message,
                in_specs=[VMEM] * 4,
                out_specs=VMEM,
                scratch_shapes=[token_scratch, best_scratch],
            )(packed, near_best, gallery_b, gallery_c)
        else:
            packed = jnp.concatenate([packed, other], axis=0)
            order = order + flips
        bit *= 2

    while bit > 1:
        bit //= 2
        arrived = swap(far, (bit * parts) | 1)
        best = jnp.maximum(near, arrived)
        near, far = best[: bit // 2], best[bit // 2 :]
    best = best[0]
    bit = parts // 2
    while bit > 1:
        best = jnp.maximum(best, swap(best, mask_of(bit)))
        bit //= 2
    return pl.pallas_call(
        functools.partial(finish_kernel, query_count, cand, tokens),
        out_shape=jax.ShapeDtypeStruct((query_count, cand), jnp.float32),
        in_specs=[VMEM, VMEM],
        out_specs=VMEM,
        compiler_params=pltpu.CompilerParams(vmem_limit_bytes=8 << 20),
        name="finish",
    )(best, swap(best, 1))


def solution(mesh):
    in_specs = (
        P(("groups", "pages"), "patches", None),
        P(("groups", "pages"), "patches", None),
        P("groups"),
        P(("groups", "pages"), None),
    )
    out_specs = P(("groups", "pages"), None)
    return jax.shard_map(body, mesh=mesh, in_specs=in_specs, out_specs=out_specs, check_vma=False)
```

```python
import functools

import jax
import jax.numpy as jnp
from jax import lax
from jax.experimental import pallas as pl
from jax.experimental.pallas import tpu as pltpu
from jax.sharding import PartitionSpec as P

LANES = 128
SUBLANES = 8
BASE = 128
INFO = 8
GROUP_PAGES = 16
UNROLLED = 3
LOADS = 4
GROUP = ("pages", "patches")
VMEM = pl.BlockSpec(memory_space=pltpu.VMEM)
HBM = pl.BlockSpec(memory_space=pltpu.HBM)


def sizes(queries, cand):
    count = queries * cand
    repeat = max(1, LANES // count)
    return count, repeat, count * repeat // LANES


def start_kernel(candidates_hbm, page_rows_hbm, tokens_hbm, info_ref, tokens_ref, candidates_ref, page_rows_ref, sems):
    copies = [
        pltpu.make_async_copy(page_rows_hbm, page_rows_ref, sems.at[0]),
        pltpu.make_async_copy(candidates_hbm, candidates_ref, sems.at[1]),
        pltpu.make_async_copy(tokens_hbm, tokens_ref, sems.at[2]),
    ]
    for copy in copies:
        copy.start()
    for copy in copies:
        copy.wait()
    queries, cand = candidates_ref.shape
    pages = page_rows_ref.shape[0]
    _, repeat, blocks = sizes(queries, cand)
    table = page_rows_ref[...].reshape(1, pages).astype(jnp.float32)
    high = jnp.floor(table * (1.0 / BASE))
    low = table - high * BASE
    digits = jnp.concatenate([high, low, jnp.zeros((6, pages), jnp.float32)], axis=0)
    found = []
    for q in range(queries):
        ids = candidates_ref[q : q + 1, :]
        hit = lax.broadcasted_iota(jnp.int32, (pages, cand), 0) == ids
        found.append(
            lax.dot_general(
                digits.astype(jnp.bfloat16),
                hit.astype(jnp.float32).astype(jnp.bfloat16),
                (((1,), (0,)), ((), ())),
                preferred_element_type=jnp.float32,
            )
        )
    line = jnp.concatenate(found * repeat, axis=1)
    rows = [line[0:1, r * LANES : (r + 1) * LANES] for r in range(blocks)]
    rows += [line[1:2, r * LANES : (r + 1) * LANES] for r in range(blocks)]
    if 2 * blocks < INFO:
        rows.append(jnp.zeros((INFO - 2 * blocks, LANES), jnp.float32))
    info_ref[...] = jnp.concatenate(rows, axis=0).astype(jnp.bfloat16)


def in_hbm(x):
    return pltpu.with_memory_space_constraint(x, pltpu.HBM)


def start(candidates, page_rows, tokens):
    return pl.pallas_call(
        start_kernel,
        out_shape=(jax.ShapeDtypeStruct((INFO, LANES), jnp.bfloat16), jax.ShapeDtypeStruct(tokens.shape, tokens.dtype)),
        in_specs=[HBM, HBM, HBM],
        out_specs=(VMEM, VMEM),
        scratch_shapes=[
            pltpu.VMEM(candidates.shape, jnp.int32),
            pltpu.VMEM(page_rows.shape, jnp.int32),
            pltpu.SemaphoreType.DMA((3,)),
        ],
        compiler_params=pltpu.CompilerParams(vmem_limit_bytes=8 << 20),
        cost_estimate=pl.CostEstimate(flops=1 << 20, transcendentals=0, bytes_accessed=1 << 20),
        name="start",
    )(in_hbm(candidates), in_hbm(page_rows), in_hbm(tokens))


def load_kernel(first, gallery_hbm, out_ref, sems):
    share = out_ref.shape[0] // LOADS
    copies = [
        pltpu.make_async_copy(
            gallery_hbm.at[pl.ds(first + i * share, share)], out_ref.at[pl.ds(i * share, share)], sems.at[i]
        )
        for i in range(LOADS)
    ]
    for copy in copies:
        copy.start()
    for copy in copies:
        copy.wait()


def load(gallery, first, count):
    shape = (count, *gallery.shape[1:])
    return pl.pallas_call(
        functools.partial(load_kernel, first),
        out_shape=jax.ShapeDtypeStruct(shape, gallery.dtype),
        in_specs=[HBM],
        out_specs=VMEM,
        scratch_shapes=[pltpu.SemaphoreType.DMA((LOADS,))],
        cost_estimate=pl.CostEstimate(
            flops=0, transcendentals=0, bytes_accessed=4 * count * gallery.shape[1] * gallery.shape[2]
        ),
        compiler_params=pltpu.CompilerParams(vmem_limit_bytes=8 << 20),
    )(in_hbm(gallery))


def arrange(order, shift, packed_ref, token_ref, columns):
    dim = packed_ref.shape[1]
    piece_rows = columns // len(order)
    planes = 1 + max(plane for plane, _ in order)
    plane_rows = columns // planes
    here = lax.shift_right_logical(lax.axis_index("patches"), shift)
    double = token_ref.shape[1] // dim
    if double == 2:
        token_ref[...] = jnp.zeros_like(token_ref)
    for i, (plane, flip) in enumerate(order):
        at = plane * plane_rows + jnp.bitwise_xor(here, flip) * piece_rows
        piece = packed_ref[i * piece_rows : (i + 1) * piece_rows, :]
        for k in range(double):
            rows = pl.ds(pl.multiple_of(at + k * columns, piece_rows), piece_rows)
            token_ref[rows, k * dim : (k + 1) * dim] = piece


def scan(gallery_ref, begin, token_ref, best_ref):
    pages, patches, dim = gallery_ref.shape
    columns = best_ref.shape[1]
    double = token_ref.shape[1] // dim
    width = min(columns, 256)
    share = GROUP_PAGES // double

    def step(i, carry):
        at = i * GROUP_PAGES
        if not isinstance(i, int):
            at = pl.multiple_of(at, GROUP_PAGES)
        sides = [gallery_ref[pl.ds(at + k * share, share)].reshape(share * patches, dim) for k in range(double)]
        patch = sides[0] if double == 1 else jnp.concatenate(sides, axis=1)
        for c in range(0, columns, width):
            sims = lax.dot_general(
                patch,
                token_ref[c : c + width * double, :],
                (((1,), (1,)), ((), ())),
                preferred_element_type=jnp.float32,
            )
            top = jnp.max(sims.reshape(share, patches, width * double), axis=1)
            for k in range(double):
                best_ref[pl.ds(begin + at + k * share, share), c : c + width] = top[:, k * width : (k + 1) * width]
        return carry

    steps = pages // GROUP_PAGES
    if double == 2 and steps <= UNROLLED:
        for i in range(steps):
            step(i, 0)
    else:
        lax.fori_loop(0, steps, step, 0)


def select(order, queries, cand, packed_ref, best_ref, out_ref):
    pages, columns = best_ref.shape
    planes = 1 + max(plane for plane, _ in order)
    pieces = len(order) // planes
    plane_rows = columns // planes
    piece_rows = plane_rows // pieces
    each = piece_rows // queries
    count, repeat, blocks = sizes(queries, cand)
    held_tokens = each * pieces // repeat
    first = lax.axis_index("pages") * pages
    lane = lax.broadcasted_iota(jnp.int32, (1, LANES), 1)
    for d in range(planes):
        block = best_ref[:, d * plane_rows : (d + 1) * plane_rows]
        info = packed_ref[columns + d * INFO : columns + (d + 1) * INFO, :].astype(jnp.float32)
        for r in range(blocks):
            rows = (info[r : r + 1, :] * BASE + info[blocks + r : blocks + r + 1, :]).astype(jnp.int32)
            local = rows - first
            held = (local >= 0) & (local < pages)
            pick = (lax.broadcasted_iota(jnp.int32, (pages, LANES), 0) == local).astype(jnp.float32)
            got = lax.dot_general(
                block,
                pick,
                (((0,), (0,)), ((), ())),
                precision=lax.Precision.HIGHEST,
                preferred_element_type=jnp.float32,
            )
            owner = ((r * LANES + lane) % count) // cand
            parts = []
            for i in range(pieces):
                at = i * piece_rows
                mine = got[at : at + each, :]
                for q in range(1, queries):
                    mine = jnp.where(owner == q, got[at + q * each : at + (q + 1) * each, :], mine)
                parts.append(mine)
            mine = jnp.where(held, jnp.concatenate(parts, axis=0), -jnp.inf)
            line = mine[0:held_tokens, :]
            for k in range(1, repeat):
                line = jnp.where(lane // count == k, mine[k * held_tokens : (k + 1) * held_tokens, :], line)
            out_ref[d, r] = line


def near_first_kernel(order, shift, packed_ref, gallery_ref, gallery_hbm, best_ref, rest_ref, token_ref, sem):
    pages = gallery_hbm.shape[0]
    rest = rest_ref.shape[0]
    copy = pltpu.make_async_copy(gallery_hbm.at[pl.ds(pages - rest, rest)], rest_ref, sem)
    copy.start()
    arrange(order, shift, packed_ref, token_ref, best_ref.shape[1])
    scan(gallery_ref, 0, token_ref, best_ref)
    copy.wait()


def near_second_kernel(queries, cand, order, shift, packed_ref, first_ref, *refs):
    *gallery_refs, out_ref, token_ref, best_ref = refs
    arrange(order, shift, packed_ref, token_ref, best_ref.shape[1])
    begin = first_ref.shape[0]
    best_ref[0:begin, :] = first_ref[...]
    for ref in gallery_refs:
        scan(ref, begin, token_ref, best_ref)
        begin += ref.shape[0]
    select(order, queries, cand, packed_ref, best_ref, out_ref)


def far_kernel(queries, cand, order, shift, packed_ref, *refs):
    *gallery_refs, out_ref, token_ref, best_ref = refs
    arrange(order, shift, packed_ref, token_ref, best_ref.shape[1])
    begin = 0
    for ref in gallery_refs:
        scan(ref, begin, token_ref, best_ref)
        begin += ref.shape[0]
    select(order, queries, cand, packed_ref, best_ref, out_ref)


def finish_kernel(queries, cand, tokens, mine_ref, other_ref, scores_ref):
    count, repeat, blocks = sizes(queries, cand)
    lines = []
    for r in range(blocks):
        best = jnp.maximum(mine_ref[r], other_ref[r])
        total = jnp.sum(best, axis=0, keepdims=True)
        line = total[:, : LANES // repeat]
        for k in range(1, repeat):
            line = line + total[:, k * count : (k + 1) * count]
        lines.append(line)
    line = lines[0] if blocks == 1 else jnp.concatenate(lines, axis=1)
    for q in range(queries):
        scores_ref[q : q + 1, :] = line[:, q * cand : (q + 1) * cand] * (1.0 / tokens)


def body(queries, gallery, page_rows, candidates):
    planes = lax.axis_size("pages")
    parts = lax.axis_size("patches")
    everyone = planes * parts
    query_count, own_tokens, dim = queries.shape
    tokens = own_tokens * parts
    cand = candidates.shape[1]
    _, repeat, blocks = sizes(query_count, cand)
    pages, patches, _ = gallery.shape

    def swap(x, mask):
        return lax.ppermute(x, GROUP, [(i, i ^ mask) for i in range(everyone)])

    def mask_of(bit):
        return bit if bit == 1 else bit | 1

    info, own = start(candidates, page_rows, queries)
    rest = GROUP_PAGES * max(1, 2 * (pages // GROUP_PAGES) // 5)
    most = pages - rest
    gallery_a = load(gallery, 0, most)
    held, bit, shift = queries, 1, 0
    while held.shape[1] % SUBLANES and bit < parts:
        other = swap(held, mask_of(bit))
        upper = (lax.axis_index("patches") & bit) != 0
        held = jnp.concatenate([jnp.where(upper, other, held), jnp.where(upper, held, other)], axis=1)
        bit, shift = bit * 2, shift + 1
    pieces = held.reshape(-1, dim)
    order = [(0, 0)]

    def double_up(pieces, order, mask):
        other = swap(pieces, mask)
        mine = own.reshape(pieces.shape) if len(order) == 1 and not shift else pieces
        return jnp.concatenate([mine, other], axis=0), order + [(p, (mask % parts >> shift) ^ f) for p, f in order]

    for bit in [1 << k for k in range(max(1, shift), parts.bit_length() - 1)]:
        pieces, order = double_up(pieces, order, mask_of(bit))
    infos = info
    for bit in [1 << k for k in range(planes.bit_length() - 2)]:
        mask = (bit * parts) | 1
        split = pieces.shape[0]
        other = swap(jnp.concatenate([pieces, infos], axis=0), mask)
        pieces = jnp.concatenate([pieces, other[:split]], axis=0)
        infos = jnp.concatenate([infos, other[split:]], axis=0)
        order = order + [(p + bit, (mask % parts >> shift) ^ f) for p, f in order]
    if not shift:
        pieces, order = double_up(pieces, order, 1)
    packed = jnp.concatenate([pieces, infos], axis=0)
    mask = (planes // 2 * parts) | 1
    other = swap(packed, mask)
    flips = [(p, (mask % parts >> shift) ^ f) for p, f in order]

    columns = planes // 2 * query_count * tokens
    double = 2 if columns <= 128 else 1
    token_scratch = pltpu.VMEM((columns * double, dim * double), jnp.bfloat16)
    best_scratch = pltpu.VMEM((pages, columns), jnp.float32)
    message = jax.ShapeDtypeStruct((planes // 2, blocks, tokens // repeat, LANES), jnp.float32)

    def call(kernel, count, **kwargs):
        return pl.pallas_call(
            kernel,
            cost_estimate=pl.CostEstimate(
                flops=2 * count * patches * dim * columns, transcendentals=0, bytes_accessed=count * patches * dim * 2
            ),
            compiler_params=pltpu.CompilerParams(vmem_limit_bytes=24 << 20),
            **kwargs,
        )

    near_best, gallery_c = call(
        functools.partial(near_first_kernel, order, shift),
        most,
        out_shape=(
            jax.ShapeDtypeStruct((most, columns), jnp.float32),
            jax.ShapeDtypeStruct((rest, patches, dim), gallery.dtype),
        ),
        in_specs=[VMEM, VMEM, HBM],
        out_specs=(VMEM, VMEM),
        scratch_shapes=[token_scratch, pltpu.SemaphoreType.DMA],
    )(packed, gallery_a, in_hbm(gallery))
    far = call(
        functools.partial(far_kernel, query_count, cand, flips, shift),
        pages,
        out_shape=message,
        in_specs=[VMEM] * 3,
        out_specs=VMEM,
        scratch_shapes=[token_scratch, best_scratch],
    )(other, gallery_a, gallery_c)
    near = call(
        functools.partial(near_second_kernel, query_count, cand, order, shift),
        rest,
        out_shape=message,
        in_specs=[VMEM] * 3,
        out_specs=VMEM,
        scratch_shapes=[token_scratch, best_scratch],
    )(packed, near_best, gallery_c)
    bit = planes
    while bit > 1:
        bit //= 2
        arrived = swap(far, (bit * parts) | 1)
        best = jnp.maximum(near, arrived)
        near, far = best[: bit // 2], best[bit // 2 :]
    best = best[0]
    bit = parts // 2
    while bit > 1:
        best = jnp.maximum(best, swap(best, mask_of(bit)))
        bit //= 2
    return pl.pallas_call(
        functools.partial(finish_kernel, query_count, cand, tokens),
        out_shape=jax.ShapeDtypeStruct((query_count, cand), jnp.float32),
        in_specs=[VMEM, VMEM],
        out_specs=VMEM,
        compiler_params=pltpu.CompilerParams(vmem_limit_bytes=8 << 20),
        name="finish",
    )(best, swap(best, 1))


def solution(mesh):
    in_specs = (
        P(("groups", "pages"), "patches", None),
        P(("groups", "pages"), "patches", None),
        P("groups"),
        P(("groups", "pages"), None),
    )
    out_specs = P(("groups", "pages"), None)
    return jax.shard_map(body, mesh=mesh, in_specs=in_specs, out_specs=out_specs, check_vma=False)
```

```python
import functools

import jax
import jax.numpy as jnp
from jax import lax
from jax.experimental import pallas as pl
from jax.experimental.pallas import tpu as pltpu
from jax.sharding import PartitionSpec as P

LANES = 128
SUBLANES = 8
BASE = 128
INFO = 8
GROUP_PAGES = 16
UNROLLED = 3
LOADS = 4
GROUP = ("pages", "patches")
VMEM = pl.BlockSpec(memory_space=pltpu.VMEM)
HBM = pl.BlockSpec(memory_space=pltpu.HBM)


def sizes(queries, cand):
    count = queries * cand
    repeat = max(1, LANES // count)
    return count, repeat, count * repeat // LANES


def start_kernel(
    candidates_hbm, page_rows_hbm, tokens_hbm, gallery_hbm, info_ref, tokens_ref, first_ref, candidates_ref, page_rows_ref, sems
):
    copies = [
        pltpu.make_async_copy(page_rows_hbm, page_rows_ref, sems.at[0]),
        pltpu.make_async_copy(candidates_hbm, candidates_ref, sems.at[1]),
        pltpu.make_async_copy(tokens_hbm, tokens_ref, sems.at[2]),
        pltpu.make_async_copy(gallery_hbm.at[pl.ds(0, first_ref.shape[0])], first_ref, sems.at[3]),
    ]
    for copy in copies:
        copy.start()
    for copy in copies[:2]:
        copy.wait()
    queries, cand = candidates_ref.shape
    pages = page_rows_ref.shape[0]
    _, repeat, blocks = sizes(queries, cand)
    table = page_rows_ref[...].reshape(1, pages).astype(jnp.float32)
    high = jnp.floor(table * (1.0 / BASE))
    low = table - high * BASE
    digits = jnp.concatenate([high, low, jnp.zeros((6, pages), jnp.float32)], axis=0)
    found = []
    for q in range(queries):
        ids = candidates_ref[q : q + 1, :]
        hit = lax.broadcasted_iota(jnp.int32, (pages, cand), 0) == ids
        found.append(
            lax.dot_general(
                digits.astype(jnp.bfloat16),
                hit.astype(jnp.float32).astype(jnp.bfloat16),
                (((1,), (0,)), ((), ())),
                preferred_element_type=jnp.float32,
            )
        )
    line = jnp.concatenate(found * repeat, axis=1)
    rows = [line[0:1, r * LANES : (r + 1) * LANES] for r in range(blocks)]
    rows += [line[1:2, r * LANES : (r + 1) * LANES] for r in range(blocks)]
    if 2 * blocks < INFO:
        rows.append(jnp.zeros((INFO - 2 * blocks, LANES), jnp.float32))
    info_ref[...] = jnp.concatenate(rows, axis=0).astype(jnp.bfloat16)
    for copy in copies[2:]:
        copy.wait()


def in_hbm(x):
    return pltpu.with_memory_space_constraint(x, pltpu.HBM)


def start(candidates, page_rows, tokens, gallery, first):
    return pl.pallas_call(
        start_kernel,
        out_shape=(
            jax.ShapeDtypeStruct((INFO, LANES), jnp.bfloat16),
            jax.ShapeDtypeStruct(tokens.shape, tokens.dtype),
            jax.ShapeDtypeStruct((first, *gallery.shape[1:]), gallery.dtype),
        ),
        in_specs=[HBM] * 4,
        out_specs=(VMEM, VMEM, VMEM),
        scratch_shapes=[
            pltpu.VMEM(candidates.shape, jnp.int32),
            pltpu.VMEM(page_rows.shape, jnp.int32),
            pltpu.SemaphoreType.DMA((4,)),
        ],
        compiler_params=pltpu.CompilerParams(vmem_limit_bytes=8 << 20),
        cost_estimate=pl.CostEstimate(flops=1 << 20, transcendentals=0, bytes_accessed=1 << 20),
        name="start",
    )(in_hbm(candidates), in_hbm(page_rows), in_hbm(tokens), in_hbm(gallery))


def load_kernel(first, gallery_hbm, out_ref, sems):
    share = out_ref.shape[0] // LOADS
    copies = [
        pltpu.make_async_copy(
            gallery_hbm.at[pl.ds(first + i * share, share)], out_ref.at[pl.ds(i * share, share)], sems.at[i]
        )
        for i in range(LOADS)
    ]
    for copy in copies:
        copy.start()
    for copy in copies:
        copy.wait()


def load(gallery, first, count):
    shape = (count, *gallery.shape[1:])
    return pl.pallas_call(
        functools.partial(load_kernel, first),
        out_shape=jax.ShapeDtypeStruct(shape, gallery.dtype),
        in_specs=[HBM],
        out_specs=VMEM,
        scratch_shapes=[pltpu.SemaphoreType.DMA((LOADS,))],
        cost_estimate=pl.CostEstimate(
            flops=0, transcendentals=0, bytes_accessed=4 * count * gallery.shape[1] * gallery.shape[2]
        ),
        compiler_params=pltpu.CompilerParams(vmem_limit_bytes=8 << 20),
    )(in_hbm(gallery))


def arrange(order, shift, packed_ref, token_ref, columns):
    dim = packed_ref.shape[1]
    piece_rows = columns // len(order)
    planes = 1 + max(plane for plane, _ in order)
    plane_rows = columns // planes
    here = lax.shift_right_logical(lax.axis_index("patches"), shift)
    double = token_ref.shape[1] // dim
    if double == 2:
        token_ref[...] = jnp.zeros_like(token_ref)
    for i, (plane, flip) in enumerate(order):
        at = plane * plane_rows + jnp.bitwise_xor(here, flip) * piece_rows
        piece = packed_ref[i * piece_rows : (i + 1) * piece_rows, :]
        for k in range(double):
            rows = pl.ds(pl.multiple_of(at + k * columns, piece_rows), piece_rows)
            token_ref[rows, k * dim : (k + 1) * dim] = piece


def scan(gallery_ref, begin, token_ref, best_ref):
    pages, patches, dim = gallery_ref.shape
    columns = best_ref.shape[1]
    double = token_ref.shape[1] // dim
    width = min(columns, 256)
    share = GROUP_PAGES // double

    def step(i, carry):
        at = i * GROUP_PAGES
        if not isinstance(i, int):
            at = pl.multiple_of(at, GROUP_PAGES)
        sides = [gallery_ref[pl.ds(at + k * share, share)].reshape(share * patches, dim) for k in range(double)]
        patch = sides[0] if double == 1 else jnp.concatenate(sides, axis=1)
        for c in range(0, columns, width):
            sims = lax.dot_general(
                patch,
                token_ref[c : c + width * double, :],
                (((1,), (1,)), ((), ())),
                preferred_element_type=jnp.float32,
            )
            top = jnp.max(sims.reshape(share, patches, width * double), axis=1)
            for k in range(double):
                best_ref[pl.ds(begin + at + k * share, share), c : c + width] = top[:, k * width : (k + 1) * width]
        return carry

    steps = pages // GROUP_PAGES
    if double == 2 and steps <= UNROLLED:
        for i in range(steps):
            step(i, 0)
    else:
        lax.fori_loop(0, steps, step, 0)


def select(order, queries, cand, packed_ref, best_ref, out_ref):
    pages, columns = best_ref.shape
    planes = 1 + max(plane for plane, _ in order)
    pieces = len(order) // planes
    plane_rows = columns // planes
    piece_rows = plane_rows // pieces
    each = piece_rows // queries
    count, repeat, blocks = sizes(queries, cand)
    held_tokens = each * pieces // repeat
    first = lax.axis_index("pages") * pages
    lane = lax.broadcasted_iota(jnp.int32, (1, LANES), 1)
    for d in range(planes):
        left = best_ref[:, d * plane_rows : (d + 1) * plane_rows]
        digits = []
        for _ in range(3):
            digits.append(left.astype(jnp.bfloat16))
            left = left - digits[-1].astype(jnp.float32)
        block = jnp.concatenate(digits, axis=0)
        info = packed_ref[columns + d * INFO : columns + (d + 1) * INFO, :].astype(jnp.float32)
        for r in range(blocks):
            rows = (info[r : r + 1, :] * BASE + info[blocks + r : blocks + r + 1, :]).astype(jnp.int32)
            local = rows - first
            held = (local >= 0) & (local < pages)
            pick = (lax.broadcasted_iota(jnp.int32, (pages, LANES), 0) == local).astype(jnp.float32)
            pick = pick.astype(jnp.bfloat16)
            got = lax.dot_general(
                block,
                jnp.concatenate([pick] * 3, axis=0),
                (((0,), (0,)), ((), ())),
                preferred_element_type=jnp.float32,
            )
            owner = ((r * LANES + lane) % count) // cand
            parts = []
            for i in range(pieces):
                at = i * piece_rows
                mine = got[at : at + each, :]
                for q in range(1, queries):
                    mine = jnp.where(owner == q, got[at + q * each : at + (q + 1) * each, :], mine)
                parts.append(mine)
            mine = jnp.where(held, jnp.concatenate(parts, axis=0), -jnp.inf)
            line = mine[0:held_tokens, :]
            for k in range(1, repeat):
                line = jnp.where(lane // count == k, mine[k * held_tokens : (k + 1) * held_tokens, :], line)
            out_ref[d, r] = line


def near_first_kernel(order, shift, packed_ref, gallery_ref, gallery_hbm, best_ref, rest_ref, token_ref, sem):
    pages = gallery_hbm.shape[0]
    rest = rest_ref.shape[0]
    copy = pltpu.make_async_copy(gallery_hbm.at[pl.ds(pages - rest, rest)], rest_ref, sem)
    copy.start()
    arrange(order, shift, packed_ref, token_ref, best_ref.shape[1])
    scan(gallery_ref, 0, token_ref, best_ref)
    copy.wait()


def near_second_kernel(queries, cand, order, shift, packed_ref, first_ref, *refs):
    *gallery_refs, out_ref, token_ref, best_ref = refs
    arrange(order, shift, packed_ref, token_ref, best_ref.shape[1])
    begin = first_ref.shape[0]
    best_ref[0:begin, :] = first_ref[...]
    for ref in gallery_refs:
        scan(ref, begin, token_ref, best_ref)
        begin += ref.shape[0]
    select(order, queries, cand, packed_ref, best_ref, out_ref)


def far_kernel(queries, cand, order, shift, packed_ref, *refs):
    *gallery_refs, out_ref, token_ref, best_ref = refs
    arrange(order, shift, packed_ref, token_ref, best_ref.shape[1])
    begin = 0
    for ref in gallery_refs:
        scan(ref, begin, token_ref, best_ref)
        begin += ref.shape[0]
    select(order, queries, cand, packed_ref, best_ref, out_ref)


def finish_kernel(queries, cand, tokens, mine_ref, other_ref, scores_ref):
    count, repeat, blocks = sizes(queries, cand)
    lines = []
    for r in range(blocks):
        best = jnp.maximum(mine_ref[r], other_ref[r])
        total = jnp.sum(best, axis=0, keepdims=True)
        line = total[:, : LANES // repeat]
        for k in range(1, repeat):
            line = line + total[:, k * count : (k + 1) * count]
        lines.append(line)
    line = lines[0] if blocks == 1 else jnp.concatenate(lines, axis=1)
    for q in range(queries):
        scores_ref[q : q + 1, :] = line[:, q * cand : (q + 1) * cand] * (1.0 / tokens)


def body(queries, gallery, page_rows, candidates):
    planes = lax.axis_size("pages")
    parts = lax.axis_size("patches")
    everyone = planes * parts
    query_count, own_tokens, dim = queries.shape
    tokens = own_tokens * parts
    cand = candidates.shape[1]
    _, repeat, blocks = sizes(query_count, cand)
    pages, patches, _ = gallery.shape

    def swap(x, mask):
        return lax.ppermute(x, GROUP, [(i, i ^ mask) for i in range(everyone)])

    def mask_of(bit):
        return bit if bit == 1 else bit | 1

    last = GROUP_PAGES * max(1, pages // GROUP_PAGES // 5)
    first = GROUP_PAGES * ((pages - last) // GROUP_PAGES // 2)
    middle = pages - first - last
    info, own, gallery_a = start(candidates, page_rows, queries, gallery, first)
    gallery_b = load(gallery, first, middle)
    held, bit, shift = queries, 1, 0
    while held.shape[1] % SUBLANES and bit < parts:
        other = swap(held, mask_of(bit))
        upper = (lax.axis_index("patches") & bit) != 0
        held = jnp.concatenate([jnp.where(upper, other, held), jnp.where(upper, held, other)], axis=1)
        bit, shift = bit * 2, shift + 1
    pieces = held.reshape(-1, dim)
    order = [(0, 0)]

    def double_up(pieces, order, mask):
        other = swap(pieces, mask)
        mine = own.reshape(pieces.shape) if len(order) == 1 and not shift else pieces
        return jnp.concatenate([mine, other], axis=0), order + [(p, (mask % parts >> shift) ^ f) for p, f in order]

    for bit in [1 << k for k in range(max(1, shift), parts.bit_length() - 1)]:
        pieces, order = double_up(pieces, order, mask_of(bit))
    infos = info
    for bit in [1 << k for k in range(planes.bit_length() - 2)]:
        mask = (bit * parts) | 1
        split = pieces.shape[0]
        other = swap(jnp.concatenate([pieces, infos], axis=0), mask)
        pieces = jnp.concatenate([pieces, other[:split]], axis=0)
        infos = jnp.concatenate([infos, other[split:]], axis=0)
        order = order + [(p + bit, (mask % parts >> shift) ^ f) for p, f in order]
    if not shift:
        pieces, order = double_up(pieces, order, 1)
    packed = jnp.concatenate([pieces, infos], axis=0)
    mask = (planes // 2 * parts) | 1
    other = swap(packed, mask)
    flips = [(p, (mask % parts >> shift) ^ f) for p, f in order]

    columns = planes // 2 * query_count * tokens
    double = 2 if columns <= 128 else 1
    token_scratch = pltpu.VMEM((columns * double, dim * double), jnp.bfloat16)
    best_scratch = pltpu.VMEM((pages, columns), jnp.float32)
    message = jax.ShapeDtypeStruct((planes // 2, blocks, tokens // repeat, LANES), jnp.float32)

    def call(kernel, count, **kwargs):
        return pl.pallas_call(
            kernel,
            cost_estimate=pl.CostEstimate(
                flops=2 * count * patches * dim * columns, transcendentals=0, bytes_accessed=count * patches * dim * 2
            ),
            compiler_params=pltpu.CompilerParams(vmem_limit_bytes=24 << 20),
            **kwargs,
        )

    near_best, gallery_c = call(
        functools.partial(near_first_kernel, order, shift),
        first,
        out_shape=(
            jax.ShapeDtypeStruct((first, columns), jnp.float32),
            jax.ShapeDtypeStruct((last, patches, dim), gallery.dtype),
        ),
        in_specs=[VMEM, VMEM, HBM],
        out_specs=(VMEM, VMEM),
        scratch_shapes=[token_scratch, pltpu.SemaphoreType.DMA],
    )(packed, gallery_a, in_hbm(gallery))
    far = call(
        functools.partial(far_kernel, query_count, cand, flips, shift),
        pages,
        out_shape=message,
        in_specs=[VMEM] * 4,
        out_specs=VMEM,
        scratch_shapes=[token_scratch, best_scratch],
    )(other, gallery_a, gallery_b, gallery_c)
    near = call(
        functools.partial(near_second_kernel, query_count, cand, order, shift),
        pages - first,
        out_shape=message,
        in_specs=[VMEM] * 4,
        out_specs=VMEM,
        scratch_shapes=[token_scratch, best_scratch],
    )(packed, near_best, gallery_b, gallery_c)
    bit = planes
    while bit > 1:
        bit //= 2
        arrived = swap(far, (bit * parts) | 1)
        best = jnp.maximum(near, arrived)
        near, far = best[: bit // 2], best[bit // 2 :]
    best = best[0]
    bit = parts // 2
    while bit > 1:
        best = jnp.maximum(best, swap(best, mask_of(bit)))
        bit //= 2
    return pl.pallas_call(
        functools.partial(finish_kernel, query_count, cand, tokens),
        out_shape=jax.ShapeDtypeStruct((query_count, cand), jnp.float32),
        in_specs=[VMEM, VMEM],
        out_specs=VMEM,
        compiler_params=pltpu.CompilerParams(vmem_limit_bytes=8 << 20),
        name="finish",
    )(best, swap(best, 1))


def solution(mesh):
    in_specs = (
        P(("groups", "pages"), "patches", None),
        P(("groups", "pages"), "patches", None),
        P("groups"),
        P(("groups", "pages"), None),
    )
    out_specs = P(("groups", "pages"), None)
    return jax.shard_map(body, mesh=mesh, in_specs=in_specs, out_specs=out_specs, check_vma=False)
```

```python
import functools

import jax
import jax.numpy as jnp
from jax import lax
from jax.experimental import pallas as pl
from jax.experimental.pallas import tpu as pltpu
from jax.sharding import PartitionSpec as P

LANES = 128
SUBLANES = 8
BASE = 128
INFO = 8
GROUP_PAGES = 16
UNROLLED = 3
LOADS = 4
GROUP = ("pages", "patches")
VMEM = pl.BlockSpec(memory_space=pltpu.VMEM)
HBM = pl.BlockSpec(memory_space=pltpu.HBM)


def sizes(queries, cand):
    count = queries * cand
    repeat = max(1, LANES // count)
    return count, repeat, count * repeat // LANES


def start_kernel(
    candidates_hbm, page_rows_hbm, tokens_hbm, gallery_hbm, info_ref, tokens_ref, first_ref, candidates_ref, page_rows_ref, sems
):
    copies = [
        pltpu.make_async_copy(page_rows_hbm, page_rows_ref, sems.at[0]),
        pltpu.make_async_copy(candidates_hbm, candidates_ref, sems.at[1]),
        pltpu.make_async_copy(tokens_hbm, tokens_ref, sems.at[2]),
        pltpu.make_async_copy(gallery_hbm.at[pl.ds(0, first_ref.shape[0])], first_ref, sems.at[3]),
    ]
    for copy in copies:
        copy.start()
    for copy in copies[:2]:
        copy.wait()
    queries, cand = candidates_ref.shape
    pages = page_rows_ref.shape[0]
    _, repeat, blocks = sizes(queries, cand)
    table = page_rows_ref[...].reshape(1, pages).astype(jnp.float32)
    high = jnp.floor(table * (1.0 / BASE))
    low = table - high * BASE
    digits = jnp.concatenate([high, low, jnp.zeros((6, pages), jnp.float32)], axis=0)
    found = []
    for q in range(queries):
        ids = candidates_ref[q : q + 1, :]
        hit = lax.broadcasted_iota(jnp.int32, (pages, cand), 0) == ids
        found.append(
            lax.dot_general(
                digits.astype(jnp.bfloat16),
                hit.astype(jnp.float32).astype(jnp.bfloat16),
                (((1,), (0,)), ((), ())),
                preferred_element_type=jnp.float32,
            )
        )
    line = jnp.concatenate(found * repeat, axis=1)
    rows = [line[0:1, r * LANES : (r + 1) * LANES] for r in range(blocks)]
    rows += [line[1:2, r * LANES : (r + 1) * LANES] for r in range(blocks)]
    if 2 * blocks < INFO:
        rows.append(jnp.zeros((INFO - 2 * blocks, LANES), jnp.float32))
    info_ref[...] = jnp.concatenate(rows, axis=0).astype(jnp.bfloat16)
    for copy in copies[2:]:
        copy.wait()


def in_hbm(x):
    return pltpu.with_memory_space_constraint(x, pltpu.HBM)


def start(candidates, page_rows, tokens, gallery, first):
    return pl.pallas_call(
        start_kernel,
        out_shape=(
            jax.ShapeDtypeStruct((INFO, LANES), jnp.bfloat16),
            jax.ShapeDtypeStruct(tokens.shape, tokens.dtype),
            jax.ShapeDtypeStruct((first, *gallery.shape[1:]), gallery.dtype),
        ),
        in_specs=[HBM] * 4,
        out_specs=(VMEM, VMEM, VMEM),
        scratch_shapes=[
            pltpu.VMEM(candidates.shape, jnp.int32),
            pltpu.VMEM(page_rows.shape, jnp.int32),
            pltpu.SemaphoreType.DMA((4,)),
        ],
        compiler_params=pltpu.CompilerParams(vmem_limit_bytes=8 << 20),
        cost_estimate=pl.CostEstimate(flops=1 << 20, transcendentals=0, bytes_accessed=1 << 20),
        name="start",
    )(in_hbm(candidates), in_hbm(page_rows), in_hbm(tokens), in_hbm(gallery))


def load_kernel(first, gallery_hbm, out_ref, sems):
    share = out_ref.shape[0] // LOADS
    copies = [
        pltpu.make_async_copy(
            gallery_hbm.at[pl.ds(first + i * share, share)], out_ref.at[pl.ds(i * share, share)], sems.at[i]
        )
        for i in range(LOADS)
    ]
    for copy in copies:
        copy.start()
    for copy in copies:
        copy.wait()


def load(gallery, first, count):
    shape = (count, *gallery.shape[1:])
    return pl.pallas_call(
        functools.partial(load_kernel, first),
        out_shape=jax.ShapeDtypeStruct(shape, gallery.dtype),
        in_specs=[HBM],
        out_specs=VMEM,
        scratch_shapes=[pltpu.SemaphoreType.DMA((LOADS,))],
        cost_estimate=pl.CostEstimate(
            flops=0, transcendentals=0, bytes_accessed=4 * count * gallery.shape[1] * gallery.shape[2]
        ),
        compiler_params=pltpu.CompilerParams(vmem_limit_bytes=8 << 20),
    )(in_hbm(gallery))


def arrange(order, shift, packed_ref, token_ref, columns):
    dim = packed_ref.shape[1]
    piece_rows = columns // len(order)
    planes = 1 + max(plane for plane, _ in order)
    plane_rows = columns // planes
    here = lax.shift_right_logical(lax.axis_index("patches"), shift)
    double = token_ref.shape[1] // dim
    if double == 2:
        token_ref[...] = jnp.zeros_like(token_ref)
    for i, (plane, flip) in enumerate(order):
        at = plane * plane_rows + jnp.bitwise_xor(here, flip) * piece_rows
        piece = packed_ref[i * piece_rows : (i + 1) * piece_rows, :]
        for k in range(double):
            rows = pl.ds(pl.multiple_of(at + k * columns, piece_rows), piece_rows)
            token_ref[rows, k * dim : (k + 1) * dim] = piece


def scan(gallery_ref, begin, token_ref, best_ref):
    pages, patches, dim = gallery_ref.shape
    columns = best_ref.shape[1]
    double = token_ref.shape[1] // dim
    width = min(columns, 256)
    share = GROUP_PAGES // double

    def step(i, carry):
        at = i * GROUP_PAGES
        if not isinstance(i, int):
            at = pl.multiple_of(at, GROUP_PAGES)
        sides = [gallery_ref[pl.ds(at + k * share, share)].reshape(share * patches, dim) for k in range(double)]
        patch = sides[0] if double == 1 else jnp.concatenate(sides, axis=1)
        for c in range(0, columns, width):
            sims = lax.dot_general(
                patch,
                token_ref[c : c + width * double, :],
                (((1,), (1,)), ((), ())),
                preferred_element_type=jnp.float32,
            )
            top = jnp.max(sims.reshape(share, patches, width * double), axis=1)
            for k in range(double):
                best_ref[pl.ds(begin + at + k * share, share), c : c + width] = top[:, k * width : (k + 1) * width]
        return carry

    steps = pages // GROUP_PAGES
    if double == 2 and steps <= UNROLLED:
        for i in range(steps):
            step(i, 0)
    else:
        lax.fori_loop(0, steps, step, 0)


def select(order, queries, cand, packed_ref, best_ref, out_ref):
    pages, columns = best_ref.shape
    planes = 1 + max(plane for plane, _ in order)
    pieces = len(order) // planes
    plane_rows = columns // planes
    piece_rows = plane_rows // pieces
    each = piece_rows // queries
    count, repeat, blocks = sizes(queries, cand)
    held_tokens = each * pieces // repeat
    first = lax.axis_index("pages") * pages
    lane = lax.broadcasted_iota(jnp.int32, (1, LANES), 1)
    for d in range(planes):
        left = best_ref[:, d * plane_rows : (d + 1) * plane_rows]
        digits = []
        for _ in range(3):
            digits.append(left.astype(jnp.bfloat16))
            left = left - digits[-1].astype(jnp.float32)
        block = jnp.concatenate(digits, axis=0)
        info = packed_ref[columns + d * INFO : columns + (d + 1) * INFO, :].astype(jnp.float32)
        for r in range(blocks):
            rows = (info[r : r + 1, :] * BASE + info[blocks + r : blocks + r + 1, :]).astype(jnp.int32)
            local = rows - first
            held = (local >= 0) & (local < pages)
            pick = (lax.broadcasted_iota(jnp.int32, (pages, LANES), 0) == local).astype(jnp.float32)
            pick = pick.astype(jnp.bfloat16)
            got = lax.dot_general(
                block,
                jnp.concatenate([pick] * 3, axis=0),
                (((0,), (0,)), ((), ())),
                preferred_element_type=jnp.float32,
            )
            owner = ((r * LANES + lane) % count) // cand
            parts = []
            for i in range(pieces):
                at = i * piece_rows
                mine = got[at : at + each, :]
                for q in range(1, queries):
                    mine = jnp.where(owner == q, got[at + q * each : at + (q + 1) * each, :], mine)
                parts.append(mine)
            mine = jnp.where(held, jnp.concatenate(parts, axis=0), -jnp.inf)
            line = mine[0:held_tokens, :]
            for k in range(1, repeat):
                line = jnp.where(lane // count == k, mine[k * held_tokens : (k + 1) * held_tokens, :], line)
            out_ref[d, r] = line


def near_first_kernel(order, shift, packed_ref, gallery_ref, gallery_hbm, best_ref, rest_ref, token_ref, sem):
    pages = gallery_hbm.shape[0]
    rest = rest_ref.shape[0]
    copy = pltpu.make_async_copy(gallery_hbm.at[pl.ds(pages - rest, rest)], rest_ref, sem)
    copy.start()
    arrange(order, shift, packed_ref, token_ref, best_ref.shape[1])
    scan(gallery_ref, 0, token_ref, best_ref)
    copy.wait()


def near_second_kernel(queries, cand, order, shift, packed_ref, first_ref, *refs):
    *gallery_refs, out_ref, token_ref, best_ref = refs
    arrange(order, shift, packed_ref, token_ref, best_ref.shape[1])
    begin = first_ref.shape[0]
    best_ref[0:begin, :] = first_ref[...]
    for ref in gallery_refs:
        scan(ref, begin, token_ref, best_ref)
        begin += ref.shape[0]
    select(order, queries, cand, packed_ref, best_ref, out_ref)


def far_kernel(queries, cand, order, shift, packed_ref, *refs):
    *gallery_refs, out_ref, token_ref, best_ref = refs
    arrange(order, shift, packed_ref, token_ref, best_ref.shape[1])
    begin = 0
    for ref in gallery_refs:
        scan(ref, begin, token_ref, best_ref)
        begin += ref.shape[0]
    select(order, queries, cand, packed_ref, best_ref, out_ref)


def finish_kernel(queries, cand, tokens, mine_ref, other_ref, scores_ref):
    count, repeat, blocks = sizes(queries, cand)
    lines = []
    for r in range(blocks):
        best = jnp.maximum(mine_ref[r], other_ref[r])
        total = jnp.sum(best, axis=0, keepdims=True)
        line = total[:, : LANES // repeat]
        for k in range(1, repeat):
            line = line + total[:, k * count : (k + 1) * count]
        lines.append(line)
    line = lines[0] if blocks == 1 else jnp.concatenate(lines, axis=1)
    for q in range(queries):
        scores_ref[q : q + 1, :] = line[:, q * cand : (q + 1) * cand] * (1.0 / tokens)


def body(queries, gallery, page_rows, candidates):
    planes = lax.axis_size("pages")
    parts = lax.axis_size("patches")
    everyone = planes * parts
    query_count, own_tokens, dim = queries.shape
    tokens = own_tokens * parts
    cand = candidates.shape[1]
    _, repeat, blocks = sizes(query_count, cand)
    pages, patches, _ = gallery.shape

    def swap(x, mask):
        return lax.ppermute(x, GROUP, [(i, i ^ mask) for i in range(everyone)])

    def mask_of(bit):
        return bit if bit == 1 else bit | 1

    last = GROUP_PAGES * max(1, pages // GROUP_PAGES // 5)
    first = GROUP_PAGES * ((pages - last) // GROUP_PAGES // 2)
    middle = pages - first - last
    info, own, gallery_a = start(candidates, page_rows, queries, gallery, first)
    gallery_b = load(gallery, first, middle)
    held, bit, shift = queries, 1, 0
    while held.shape[1] % SUBLANES and bit < parts:
        other = swap(held, mask_of(bit))
        upper = (lax.axis_index("patches") & bit) != 0
        held = jnp.concatenate([jnp.where(upper, other, held), jnp.where(upper, held, other)], axis=1)
        bit, shift = bit * 2, shift + 1
    pieces = held.reshape(-1, dim)
    order = [(0, 0)]

    def double_up(pieces, order, mask):
        other = swap(pieces, mask)
        mine = own.reshape(pieces.shape) if len(order) == 1 and not shift else pieces
        return jnp.concatenate([mine, other], axis=0), order + [(p, (mask % parts >> shift) ^ f) for p, f in order]

    for bit in [1 << k for k in range(max(1, shift), parts.bit_length() - 1)]:
        pieces, order = double_up(pieces, order, mask_of(bit))
    infos = info
    hops = [1 << k for k in reversed(range(planes.bit_length() - 1))]
    for bit in hops[:-1]:
        mask = (bit * parts) | 1
        known = infos.shape[0] // INFO
        split = pieces.shape[0]
        other = swap(jnp.concatenate([pieces, infos], axis=0), mask)
        pieces = jnp.concatenate([pieces, other[:split]], axis=0)
        infos = jnp.concatenate([infos, other[split:]], axis=0)
        order = order + [(p + known, (mask % parts >> shift) ^ f) for p, f in order]
    if not shift:
        pieces, order = double_up(pieces, order, 1)
    packed = jnp.concatenate([pieces, infos], axis=0)
    mask = (hops[-1] * parts) | 1
    other = swap(packed, mask)
    flips = [(p, (mask % parts >> shift) ^ f) for p, f in order]

    columns = planes // 2 * query_count * tokens
    double = 2 if columns <= 128 else 1
    token_scratch = pltpu.VMEM((columns * double, dim * double), jnp.bfloat16)
    best_scratch = pltpu.VMEM((pages, columns), jnp.float32)
    message = jax.ShapeDtypeStruct((planes // 2, blocks, tokens // repeat, LANES), jnp.float32)

    def call(kernel, count, **kwargs):
        return pl.pallas_call(
            kernel,
            cost_estimate=pl.CostEstimate(
                flops=2 * count * patches * dim * columns, transcendentals=0, bytes_accessed=count * patches * dim * 2
            ),
            compiler_params=pltpu.CompilerParams(vmem_limit_bytes=24 << 20),
            **kwargs,
        )

    near_best, gallery_c = call(
        functools.partial(near_first_kernel, order, shift),
        first,
        out_shape=(
            jax.ShapeDtypeStruct((first, columns), jnp.float32),
            jax.ShapeDtypeStruct((last, patches, dim), gallery.dtype),
        ),
        in_specs=[VMEM, VMEM, HBM],
        out_specs=(VMEM, VMEM),
        scratch_shapes=[token_scratch, pltpu.SemaphoreType.DMA],
    )(packed, gallery_a, in_hbm(gallery))
    far = call(
        functools.partial(far_kernel, query_count, cand, flips, shift),
        pages,
        out_shape=message,
        in_specs=[VMEM] * 4,
        out_specs=VMEM,
        scratch_shapes=[token_scratch, best_scratch],
    )(other, gallery_a, gallery_b, gallery_c)
    near = call(
        functools.partial(near_second_kernel, query_count, cand, order, shift),
        pages - first,
        out_shape=message,
        in_specs=[VMEM] * 4,
        out_specs=VMEM,
        scratch_shapes=[token_scratch, best_scratch],
    )(packed, near_best, gallery_b, gallery_c)
    for bit in reversed(hops):
        arrived = swap(far, (bit * parts) | 1)
        best = jnp.maximum(near, arrived)
        half = best.shape[0] // 2
        near, far = best[:half], best[half:]
    best = best[0]
    bit = parts // 2
    while bit > 1:
        best = jnp.maximum(best, swap(best, mask_of(bit)))
        bit //= 2
    return pl.pallas_call(
        functools.partial(finish_kernel, query_count, cand, tokens),
        out_shape=jax.ShapeDtypeStruct((query_count, cand), jnp.float32),
        in_specs=[VMEM, VMEM],
        out_specs=VMEM,
        compiler_params=pltpu.CompilerParams(vmem_limit_bytes=8 << 20),
        name="finish",
    )(best, swap(best, 1))


def solution(mesh):
    in_specs = (
        P(("groups", "pages"), "patches", None),
        P(("groups", "pages"), "patches", None),
        P("groups"),
        P(("groups", "pages"), None),
    )
    out_specs = P(("groups", "pages"), None)
    return jax.shard_map(body, mesh=mesh, in_specs=in_specs, out_specs=out_specs, check_vma=False)
```

```python
import functools

import jax
import jax.numpy as jnp
from jax import lax
from jax.experimental import pallas as pl
from jax.experimental.pallas import tpu as pltpu
from jax.sharding import PartitionSpec as P

LANES = 128
SUBLANES = 8
BASE = 128
INFO = 8
GROUP_PAGES = 16
UNROLLED = 3
LOADS = 4
GROUP = ("pages", "patches")
VMEM = pl.BlockSpec(memory_space=pltpu.VMEM)
HBM = pl.BlockSpec(memory_space=pltpu.HBM)


def sizes(queries, cand):
    count = queries * cand
    repeat = max(1, LANES // count)
    return count, repeat, count * repeat // LANES


def start_kernel(
    candidates_hbm, page_rows_hbm, tokens_hbm, gallery_hbm, info_ref, tokens_ref, first_ref, candidates_ref, page_rows_ref, sems
):
    copies = [
        pltpu.make_async_copy(page_rows_hbm, page_rows_ref, sems.at[0]),
        pltpu.make_async_copy(candidates_hbm, candidates_ref, sems.at[1]),
        pltpu.make_async_copy(tokens_hbm, tokens_ref, sems.at[2]),
        pltpu.make_async_copy(gallery_hbm.at[pl.ds(0, first_ref.shape[0])], first_ref, sems.at[3]),
    ]
    for copy in copies:
        copy.start()
    for copy in copies[:2]:
        copy.wait()
    queries, cand = candidates_ref.shape
    pages = page_rows_ref.shape[0]
    _, repeat, blocks = sizes(queries, cand)
    table = page_rows_ref[...].reshape(1, pages).astype(jnp.float32)
    high = jnp.floor(table * (1.0 / BASE))
    low = table - high * BASE
    digits = jnp.concatenate([high, low, jnp.zeros((6, pages), jnp.float32)], axis=0)
    found = []
    for q in range(queries):
        ids = candidates_ref[q : q + 1, :]
        hit = lax.broadcasted_iota(jnp.int32, (pages, cand), 0) == ids
        found.append(
            lax.dot_general(
                digits.astype(jnp.bfloat16),
                hit.astype(jnp.float32).astype(jnp.bfloat16),
                (((1,), (0,)), ((), ())),
                preferred_element_type=jnp.float32,
            )
        )
    line = jnp.concatenate(found * repeat, axis=1)
    rows = [line[0:1, r * LANES : (r + 1) * LANES] for r in range(blocks)]
    rows += [line[1:2, r * LANES : (r + 1) * LANES] for r in range(blocks)]
    if 2 * blocks < INFO:
        rows.append(jnp.zeros((INFO - 2 * blocks, LANES), jnp.float32))
    info_ref[...] = jnp.concatenate(rows, axis=0).astype(jnp.bfloat16)
    for copy in copies[2:]:
        copy.wait()


def in_hbm(x):
    return pltpu.with_memory_space_constraint(x, pltpu.HBM)


def start(candidates, page_rows, tokens, gallery, first):
    return pl.pallas_call(
        start_kernel,
        out_shape=(
            jax.ShapeDtypeStruct((INFO, LANES), jnp.bfloat16),
            jax.ShapeDtypeStruct(tokens.shape, tokens.dtype),
            jax.ShapeDtypeStruct((first, *gallery.shape[1:]), gallery.dtype),
        ),
        in_specs=[HBM] * 4,
        out_specs=(VMEM, VMEM, VMEM),
        scratch_shapes=[
            pltpu.VMEM(candidates.shape, jnp.int32),
            pltpu.VMEM(page_rows.shape, jnp.int32),
            pltpu.SemaphoreType.DMA((4,)),
        ],
        compiler_params=pltpu.CompilerParams(vmem_limit_bytes=8 << 20),
        cost_estimate=pl.CostEstimate(flops=1 << 20, transcendentals=0, bytes_accessed=1 << 20),
        name="start",
    )(in_hbm(candidates), in_hbm(page_rows), in_hbm(tokens), in_hbm(gallery))


def load_kernel(first, gallery_hbm, out_ref, sems):
    share = out_ref.shape[0] // LOADS
    copies = [
        pltpu.make_async_copy(
            gallery_hbm.at[pl.ds(first + i * share, share)], out_ref.at[pl.ds(i * share, share)], sems.at[i]
        )
        for i in range(LOADS)
    ]
    for copy in copies:
        copy.start()
    for copy in copies:
        copy.wait()


def load(gallery, first, count):
    shape = (count, *gallery.shape[1:])
    return pl.pallas_call(
        functools.partial(load_kernel, first),
        out_shape=jax.ShapeDtypeStruct(shape, gallery.dtype),
        in_specs=[HBM],
        out_specs=VMEM,
        scratch_shapes=[pltpu.SemaphoreType.DMA((LOADS,))],
        cost_estimate=pl.CostEstimate(
            flops=0, transcendentals=0, bytes_accessed=4 * count * gallery.shape[1] * gallery.shape[2]
        ),
        compiler_params=pltpu.CompilerParams(vmem_limit_bytes=8 << 20),
    )(in_hbm(gallery))


def arrange(order, shift, packed_refs, token_ref, columns):
    dim = packed_refs[0].shape[1]
    piece_rows = columns // len(order)
    held = columns // len(packed_refs)
    planes = 1 + max(plane for plane, _ in order)
    plane_rows = columns // planes
    here = lax.shift_right_logical(lax.axis_index("patches"), shift)
    double = token_ref.shape[1] // dim
    if double == 2:
        token_ref[:columns, dim:] = jnp.zeros((columns, dim), token_ref.dtype)
        token_ref[columns:, :dim] = jnp.zeros((columns, dim), token_ref.dtype)
    for i, (plane, flip) in enumerate(order):
        at = plane * plane_rows + jnp.bitwise_xor(here, flip) * piece_rows
        start = i * piece_rows % held
        piece = packed_refs[i * piece_rows // held][start : start + piece_rows, :]
        for k in range(double):
            rows = pl.ds(pl.multiple_of(at + k * columns, piece_rows), piece_rows)
            token_ref[rows, k * dim : (k + 1) * dim] = piece


def scan(gallery_ref, begin, token_ref, best_ref):
    pages, patches, dim = gallery_ref.shape
    columns = best_ref.shape[1]
    double = token_ref.shape[1] // dim
    width = min(columns, 256)
    share = GROUP_PAGES // double

    def step(i, carry):
        at = i * GROUP_PAGES
        if not isinstance(i, int):
            at = pl.multiple_of(at, GROUP_PAGES)
        sides = [gallery_ref[pl.ds(at + k * share, share)].reshape(share * patches, dim) for k in range(double)]
        patch = sides[0] if double == 1 else jnp.concatenate(sides, axis=1)
        for c in range(0, columns, width):
            sims = lax.dot_general(
                patch,
                token_ref[c : c + width * double, :],
                (((1,), (1,)), ((), ())),
                preferred_element_type=jnp.float32,
            )
            top = jnp.max(sims.reshape(share, patches, width * double), axis=1)
            for k in range(double):
                best_ref[pl.ds(begin + at + k * share, share), c : c + width] = top[:, k * width : (k + 1) * width]
        return carry

    steps = pages // GROUP_PAGES
    if double == 2 and steps <= UNROLLED:
        for i in range(steps):
            step(i, 0)
    else:
        lax.fori_loop(0, steps, step, 0)


def select(order, queries, cand, packed_refs, best_ref, out_ref):
    pages, columns = best_ref.shape
    info_start = columns // len(packed_refs)
    planes = 1 + max(plane for plane, _ in order)
    pieces = len(order) // planes
    plane_rows = columns // planes
    piece_rows = plane_rows // pieces
    each = piece_rows // queries
    count, repeat, blocks = sizes(queries, cand)
    held_tokens = each * pieces // repeat
    first = lax.axis_index("pages") * pages
    lane = lax.broadcasted_iota(jnp.int32, (1, LANES), 1)
    for d in range(planes):
        left = best_ref[:, d * plane_rows : (d + 1) * plane_rows]
        digits = []
        for _ in range(3):
            digits.append(left.astype(jnp.bfloat16))
            left = left - digits[-1].astype(jnp.float32)
        block = jnp.concatenate(digits, axis=0)
        info = packed_refs[0][info_start + d * INFO : info_start + (d + 1) * INFO, :].astype(jnp.float32)
        for r in range(blocks):
            rows = (info[r : r + 1, :] * BASE + info[blocks + r : blocks + r + 1, :]).astype(jnp.int32)
            local = rows - first
            held = (local >= 0) & (local < pages)
            pick = (lax.broadcasted_iota(jnp.int32, (pages, LANES), 0) == local).astype(jnp.float32)
            pick = pick.astype(jnp.bfloat16)
            got = lax.dot_general(
                block,
                jnp.concatenate([pick] * 3, axis=0),
                (((0,), (0,)), ((), ())),
                preferred_element_type=jnp.float32,
            )
            owner = ((r * LANES + lane) % count) // cand
            parts = []
            for i in range(pieces):
                at = i * piece_rows
                mine = got[at : at + each, :]
                for q in range(1, queries):
                    mine = jnp.where(owner == q, got[at + q * each : at + (q + 1) * each, :], mine)
                parts.append(mine)
            mine = jnp.where(held, jnp.concatenate(parts, axis=0), -jnp.inf)
            line = mine[0:held_tokens, :]
            for k in range(1, repeat):
                line = jnp.where(lane // count == k, mine[k * held_tokens : (k + 1) * held_tokens, :], line)
            out_ref[d, r] = line


def near_first_kernel(order, shift, count, *refs):
    packed_refs, (gallery_ref, best_ref, token_ref) = refs[:count], refs[count:]
    arrange(order, shift, packed_refs, token_ref, best_ref.shape[1])
    scan(gallery_ref, 0, token_ref, best_ref)


def near_second_kernel(queries, cand, order, shift, count, *refs):
    packed_refs, (first_ref, *gallery_refs, out_ref, token_ref, best_ref) = refs[:count], refs[count:]
    arrange(order, shift, packed_refs, token_ref, best_ref.shape[1])
    begin = 0
    for ref in gallery_refs:
        scan(ref, begin, token_ref, best_ref)
        begin += ref.shape[0]
    best_ref[begin : begin + first_ref.shape[0], :] = first_ref[...]
    select(order, queries, cand, packed_refs, best_ref, out_ref)


def far_kernel(queries, cand, order, shift, count, *refs):
    packed_refs, (*gallery_refs, out_ref, token_ref, best_ref) = refs[:count], refs[count:]
    arrange(order, shift, packed_refs, token_ref, best_ref.shape[1])
    begin = 0
    for ref in gallery_refs:
        scan(ref, begin, token_ref, best_ref)
        begin += ref.shape[0]
    select(order, queries, cand, packed_refs, best_ref, out_ref)


def finish_kernel(queries, cand, tokens, mine_ref, other_ref, scores_ref):
    count, repeat, blocks = sizes(queries, cand)
    lines = []
    for r in range(blocks):
        best = jnp.maximum(mine_ref[r], other_ref[r])
        total = jnp.sum(best, axis=0, keepdims=True)
        line = total[:, : LANES // repeat]
        for k in range(1, repeat):
            line = line + total[:, k * count : (k + 1) * count]
        lines.append(line)
    line = lines[0] if blocks == 1 else jnp.concatenate(lines, axis=1)
    for q in range(queries):
        scores_ref[q : q + 1, :] = line[:, q * cand : (q + 1) * cand] * (1.0 / tokens)


def body(queries, gallery, page_rows, candidates):
    planes = lax.axis_size("pages")
    parts = lax.axis_size("patches")
    everyone = planes * parts
    query_count, own_tokens, dim = queries.shape
    tokens = own_tokens * parts
    cand = candidates.shape[1]
    _, repeat, blocks = sizes(query_count, cand)
    pages, patches, _ = gallery.shape

    def swap(x, mask):
        return lax.ppermute(x, GROUP, [(i, i ^ mask) for i in range(everyone)])

    def mask_of(bit):
        return bit if bit == 1 else bit | 1

    last = GROUP_PAGES * max(1, pages // GROUP_PAGES // 5)
    first = GROUP_PAGES * ((pages - last) // GROUP_PAGES // 2)
    middle = pages - first - last
    info, own, gallery_a = start(candidates, page_rows, queries, gallery, first)
    gallery_b = load(gallery, first, middle)
    gallery_c = load(gallery, first + middle, last)
    held, bit, shift = queries, 1, 0
    while held.shape[1] % SUBLANES and bit < parts:
        other = swap(held, mask_of(bit))
        upper = (lax.axis_index("patches") & bit) != 0
        held = jnp.concatenate([jnp.where(upper, other, held), jnp.where(upper, held, other)], axis=1)
        bit, shift = bit * 2, shift + 1
    pieces = held.reshape(-1, dim)
    order = [(0, 0)]

    def double_up(pieces, order, mask):
        other = swap(pieces, mask)
        mine = own.reshape(pieces.shape) if len(order) == 1 and not shift else pieces
        return jnp.concatenate([mine, other], axis=0), order + [(p, (mask % parts >> shift) ^ f) for p, f in order]

    for bit in [1 << k for k in range(max(1, shift), parts.bit_length() - 1)]:
        pieces, order = double_up(pieces, order, mask_of(bit))
    infos = info
    hops = [1 << k for k in reversed(range(planes.bit_length() - 1))]
    for bit in hops[:-1]:
        mask = (bit * parts) | 1
        known = infos.shape[0] // INFO
        split = pieces.shape[0]
        other = swap(jnp.concatenate([pieces, infos], axis=0), mask)
        pieces = jnp.concatenate([pieces, other[:split]], axis=0)
        infos = jnp.concatenate([infos, other[split:]], axis=0)
        order = order + [(p + known, (mask % parts >> shift) ^ f) for p, f in order]
    mask = (hops[-1] * parts) | 1
    split = pieces.shape[0]
    sent = jnp.concatenate([pieces, infos], axis=0)
    other = swap(sent, mask)
    packed, other = [sent], [other]
    flips = [(p, (mask % parts >> shift) ^ f) for p, f in order]
    if not shift:
        packed.append(swap(pieces, 1))
        other.append(swap(other[0][:split], 1))
        order = order + [(p, 1 ^ f) for p, f in order]
        flips = flips + [(p, 1 ^ f) for p, f in flips]

    columns = planes // 2 * query_count * tokens
    double = 2 if columns <= 128 else 1
    token_scratch = pltpu.VMEM((columns * double, dim * double), jnp.bfloat16)
    best_scratch = pltpu.VMEM((pages, columns), jnp.float32)
    message = jax.ShapeDtypeStruct((planes // 2, blocks, tokens // repeat, LANES), jnp.float32)

    def call(kernel, count, **kwargs):
        return pl.pallas_call(
            kernel,
            cost_estimate=pl.CostEstimate(
                flops=2 * count * patches * dim * columns, transcendentals=0, bytes_accessed=count * patches * dim * 2
            ),
            compiler_params=pltpu.CompilerParams(vmem_limit_bytes=24 << 20),
            **kwargs,
        )

    near_best = call(
        functools.partial(near_first_kernel, order, shift, len(packed)),
        last,
        out_shape=jax.ShapeDtypeStruct((last, columns), jnp.float32),
        in_specs=[VMEM] * (len(packed) + 1),
        out_specs=VMEM,
        scratch_shapes=[token_scratch],
    )(*packed, gallery_c)
    far = call(
        functools.partial(far_kernel, query_count, cand, flips, shift, len(other)),
        pages,
        out_shape=message,
        in_specs=[VMEM] * (len(packed) + 3),
        out_specs=VMEM,
        scratch_shapes=[token_scratch, best_scratch],
    )(*other, gallery_a, gallery_b, gallery_c)
    near = call(
        functools.partial(near_second_kernel, query_count, cand, order, shift, len(packed)),
        pages - last,
        out_shape=message,
        in_specs=[VMEM] * (len(packed) + 3),
        out_specs=VMEM,
        scratch_shapes=[token_scratch, best_scratch],
    )(*packed, near_best, gallery_a, gallery_b)
    for bit in reversed(hops):
        arrived = swap(far, (bit * parts) | 1)
        best = jnp.maximum(near, arrived)
        half = best.shape[0] // 2
        near, far = best[:half], best[half:]
    best = best[0]
    bit = parts // 2
    while bit > 1:
        best = jnp.maximum(best, swap(best, mask_of(bit)))
        bit //= 2
    return pl.pallas_call(
        functools.partial(finish_kernel, query_count, cand, tokens),
        out_shape=jax.ShapeDtypeStruct((query_count, cand), jnp.float32),
        in_specs=[VMEM, VMEM],
        out_specs=VMEM,
        compiler_params=pltpu.CompilerParams(vmem_limit_bytes=8 << 20),
        name="finish",
    )(best, swap(best, 1))


def solution(mesh):
    in_specs = (
        P(("groups", "pages"), "patches", None),
        P(("groups", "pages"), "patches", None),
        P("groups"),
        P(("groups", "pages"), None),
    )
    out_specs = P(("groups", "pages"), None)
    return jax.shard_map(body, mesh=mesh, in_specs=in_specs, out_specs=out_specs, check_vma=False)
```

```python
import functools

import jax
import jax.numpy as jnp
from jax import lax
from jax.experimental import pallas as pl
from jax.experimental.pallas import tpu as pltpu
from jax.sharding import PartitionSpec as P

LANES = 128
SUBLANES = 8
BASE = 128
INFO = 8
GROUP_PAGES = 16
UNROLLED = 3
LOADS = 4
GROUP = ("pages", "patches")
VMEM = pl.BlockSpec(memory_space=pltpu.VMEM)
HBM = pl.BlockSpec(memory_space=pltpu.HBM)


def sizes(queries, cand):
    count = queries * cand
    repeat = max(1, LANES // count)
    return count, repeat, count * repeat // LANES


def start_kernel(
    candidates_hbm, page_rows_hbm, tokens_hbm, gallery_hbm, info_ref, tokens_ref, first_ref, candidates_ref, page_rows_ref, sems
):
    copies = [
        pltpu.make_async_copy(page_rows_hbm, page_rows_ref, sems.at[0]),
        pltpu.make_async_copy(candidates_hbm, candidates_ref, sems.at[1]),
        pltpu.make_async_copy(tokens_hbm, tokens_ref, sems.at[2]),
        pltpu.make_async_copy(gallery_hbm.at[pl.ds(0, first_ref.shape[0])], first_ref, sems.at[3]),
    ]
    for copy in copies:
        copy.start()
    for copy in copies[:2]:
        copy.wait()
    queries, cand = candidates_ref.shape
    pages = page_rows_ref.shape[0]
    _, repeat, blocks = sizes(queries, cand)
    table = page_rows_ref[...].reshape(1, pages).astype(jnp.float32)
    high = jnp.floor(table * (1.0 / BASE))
    low = table - high * BASE
    digits = jnp.concatenate([high, low, jnp.zeros((6, pages), jnp.float32)], axis=0)
    found = []
    for q in range(queries):
        ids = candidates_ref[q : q + 1, :]
        hit = lax.broadcasted_iota(jnp.int32, (pages, cand), 0) == ids
        found.append(
            lax.dot_general(
                digits.astype(jnp.bfloat16),
                hit.astype(jnp.float32).astype(jnp.bfloat16),
                (((1,), (0,)), ((), ())),
                preferred_element_type=jnp.float32,
            )
        )
    line = jnp.concatenate(found * repeat, axis=1)
    rows = [line[0:1, r * LANES : (r + 1) * LANES] for r in range(blocks)]
    rows += [line[1:2, r * LANES : (r + 1) * LANES] for r in range(blocks)]
    if 2 * blocks < INFO:
        rows.append(jnp.zeros((INFO - 2 * blocks, LANES), jnp.float32))
    info_ref[...] = jnp.concatenate(rows, axis=0).astype(jnp.bfloat16)
    for copy in copies[2:]:
        copy.wait()


def in_hbm(x):
    return pltpu.with_memory_space_constraint(x, pltpu.HBM)


def start(candidates, page_rows, tokens, gallery, first):
    return pl.pallas_call(
        start_kernel,
        out_shape=(
            jax.ShapeDtypeStruct((INFO, LANES), jnp.bfloat16),
            jax.ShapeDtypeStruct(tokens.shape, tokens.dtype),
            jax.ShapeDtypeStruct((first, *gallery.shape[1:]), gallery.dtype),
        ),
        in_specs=[HBM] * 4,
        out_specs=(VMEM, VMEM, VMEM),
        scratch_shapes=[
            pltpu.VMEM(candidates.shape, jnp.int32),
            pltpu.VMEM(page_rows.shape, jnp.int32),
            pltpu.SemaphoreType.DMA((4,)),
        ],
        compiler_params=pltpu.CompilerParams(vmem_limit_bytes=8 << 20),
        cost_estimate=pl.CostEstimate(flops=1 << 20, transcendentals=0, bytes_accessed=1 << 20),
        name="start",
    )(in_hbm(candidates), in_hbm(page_rows), in_hbm(tokens), in_hbm(gallery))


def load_kernel(first, gallery_hbm, out_ref, sems):
    share = out_ref.shape[0] // LOADS
    copies = [
        pltpu.make_async_copy(
            gallery_hbm.at[pl.ds(first + i * share, share)], out_ref.at[pl.ds(i * share, share)], sems.at[i]
        )
        for i in range(LOADS)
    ]
    for copy in copies:
        copy.start()
    for copy in copies:
        copy.wait()


def load(gallery, first, count):
    shape = (count, *gallery.shape[1:])
    return pl.pallas_call(
        functools.partial(load_kernel, first),
        out_shape=jax.ShapeDtypeStruct(shape, gallery.dtype),
        in_specs=[HBM],
        out_specs=VMEM,
        scratch_shapes=[pltpu.SemaphoreType.DMA((LOADS,))],
        cost_estimate=pl.CostEstimate(
            flops=0, transcendentals=0, bytes_accessed=4 * count * gallery.shape[1] * gallery.shape[2]
        ),
        compiler_params=pltpu.CompilerParams(vmem_limit_bytes=8 << 20),
    )(in_hbm(gallery))


def arrange(order, shift, packed_refs, token_ref, columns):
    dim = packed_refs[0].shape[1]
    piece_rows = columns // len(order)
    held = columns // len(packed_refs)
    planes = 1 + max(plane for plane, _ in order)
    plane_rows = columns // planes
    here = lax.shift_right_logical(lax.axis_index("patches"), shift)
    double = token_ref.shape[1] // dim
    if double == 2:
        token_ref[...] = jnp.zeros_like(token_ref)
    for i, (plane, flip) in enumerate(order):
        at = plane * plane_rows + jnp.bitwise_xor(here, flip) * piece_rows
        start = i * piece_rows % held
        piece = packed_refs[i * piece_rows // held][start : start + piece_rows, :]
        for k in range(double):
            rows = pl.ds(pl.multiple_of(at + k * columns, piece_rows), piece_rows)
            token_ref[rows, k * dim : (k + 1) * dim] = piece


def scan(gallery_ref, begin, token_ref, best_ref):
    pages, patches, dim = gallery_ref.shape
    columns = best_ref.shape[1]
    double = token_ref.shape[1] // dim
    width = min(columns, 256)
    share = GROUP_PAGES // double

    def step(i, carry):
        at = i * GROUP_PAGES
        if not isinstance(i, int):
            at = pl.multiple_of(at, GROUP_PAGES)
        sides = [gallery_ref[pl.ds(at + k * share, share)].reshape(share * patches, dim) for k in range(double)]
        patch = sides[0] if double == 1 else jnp.concatenate(sides, axis=1)
        for c in range(0, columns, width):
            sims = lax.dot_general(
                patch,
                token_ref[c : c + width * double, :],
                (((1,), (1,)), ((), ())),
                preferred_element_type=jnp.float32,
            )
            top = jnp.max(sims.reshape(share, patches, width * double), axis=1)
            for k in range(double):
                best_ref[pl.ds(begin + at + k * share, share), c : c + width] = top[:, k * width : (k + 1) * width]
        return carry

    steps = pages // GROUP_PAGES
    if double == 2 and steps <= UNROLLED:
        for i in range(steps):
            step(i, 0)
    else:
        lax.fori_loop(0, steps, step, 0)


def select(order, queries, cand, packed_refs, best_ref, out_ref):
    pages, columns = best_ref.shape
    info_start = columns // len(packed_refs)
    planes = 1 + max(plane for plane, _ in order)
    pieces = len(order) // planes
    plane_rows = columns // planes
    piece_rows = plane_rows // pieces
    each = piece_rows // queries
    count, repeat, blocks = sizes(queries, cand)
    held_tokens = each * pieces // repeat
    first = lax.axis_index("pages") * pages
    lane = lax.broadcasted_iota(jnp.int32, (1, LANES), 1)
    for d in range(planes):
        left = best_ref[:, d * plane_rows : (d + 1) * plane_rows]
        digits = []
        for _ in range(3):
            digits.append(left.astype(jnp.bfloat16))
            left = left - digits[-1].astype(jnp.float32)
        block = jnp.concatenate(digits, axis=0)
        info = packed_refs[0][info_start + d * INFO : info_start + (d + 1) * INFO, :].astype(jnp.float32)
        for r in range(blocks):
            rows = (info[r : r + 1, :] * BASE + info[blocks + r : blocks + r + 1, :]).astype(jnp.int32)
            local = rows - first
            held = (local >= 0) & (local < pages)
            pick = (lax.broadcasted_iota(jnp.int32, (pages, LANES), 0) == local).astype(jnp.float32)
            pick = pick.astype(jnp.bfloat16)
            got = lax.dot_general(
                block,
                jnp.concatenate([pick] * 3, axis=0),
                (((0,), (0,)), ((), ())),
                preferred_element_type=jnp.float32,
            )
            owner = ((r * LANES + lane) % count) // cand
            parts = []
            for i in range(pieces):
                at = i * piece_rows
                mine = got[at : at + each, :]
                for q in range(1, queries):
                    mine = jnp.where(owner == q, got[at + q * each : at + (q + 1) * each, :], mine)
                parts.append(mine)
            mine = jnp.where(held, jnp.concatenate(parts, axis=0), -jnp.inf)
            line = mine[0:held_tokens, :]
            for k in range(1, repeat):
                line = jnp.where(lane // count == k, mine[k * held_tokens : (k + 1) * held_tokens, :], line)
            out_ref[d, r] = line


def near_first_kernel(order, shift, count, *refs):
    packed_refs, (gallery_ref, best_ref, token_ref) = refs[:count], refs[count:]
    arrange(order, shift, packed_refs, token_ref, best_ref.shape[1])
    scan(gallery_ref, 0, token_ref, best_ref)


def near_second_kernel(queries, cand, order, shift, count, *refs):
    packed_refs, (first_ref, *gallery_refs, out_ref, token_ref, best_ref) = refs[:count], refs[count:]
    arrange(order, shift, packed_refs, token_ref, best_ref.shape[1])
    begin = 0
    for ref in gallery_refs:
        scan(ref, begin, token_ref, best_ref)
        begin += ref.shape[0]
    best_ref[begin : begin + first_ref.shape[0], :] = first_ref[...]
    select(order, queries, cand, packed_refs, best_ref, out_ref)


def far_kernel(queries, cand, order, shift, count, *refs):
    packed_refs, (*gallery_refs, out_ref, token_ref, best_ref) = refs[:count], refs[count:]
    arrange(order, shift, packed_refs, token_ref, best_ref.shape[1])
    begin = 0
    for ref in gallery_refs:
        scan(ref, begin, token_ref, best_ref)
        begin += ref.shape[0]
    select(order, queries, cand, packed_refs, best_ref, out_ref)


def finish_kernel(queries, cand, tokens, mine_ref, other_ref, scores_ref):
    count, repeat, blocks = sizes(queries, cand)
    lines = []
    for r in range(blocks):
        best = jnp.maximum(mine_ref[r], other_ref[r])
        total = jnp.sum(best, axis=0, keepdims=True)
        line = total[:, : LANES // repeat]
        for k in range(1, repeat):
            line = line + total[:, k * count : (k + 1) * count]
        lines.append(line)
    line = lines[0] if blocks == 1 else jnp.concatenate(lines, axis=1)
    for q in range(queries):
        scores_ref[q : q + 1, :] = line[:, q * cand : (q + 1) * cand] * (1.0 / tokens)


def body(queries, gallery, page_rows, candidates):
    planes = lax.axis_size("pages")
    parts = lax.axis_size("patches")
    everyone = planes * parts
    query_count, own_tokens, dim = queries.shape
    tokens = own_tokens * parts
    cand = candidates.shape[1]
    _, repeat, blocks = sizes(query_count, cand)
    pages, patches, _ = gallery.shape

    def swap(x, mask):
        return lax.ppermute(x, GROUP, [(i, i ^ mask) for i in range(everyone)])

    def mask_of(bit):
        return bit if bit == 1 else bit | 1

    last = GROUP_PAGES * max(1, pages // GROUP_PAGES // 5)
    first = GROUP_PAGES * ((pages - last) // GROUP_PAGES * 3 // 4)
    middle = pages - first - last
    info, own, gallery_a = start(candidates, page_rows, queries, gallery, first)
    gallery_b = load(gallery, first, middle)
    gallery_c = load(gallery, first + middle, last)
    held, bit, shift = queries, 1, 0
    while held.shape[1] % SUBLANES and bit < parts:
        other = swap(held, mask_of(bit))
        upper = (lax.axis_index("patches") & bit) != 0
        held = jnp.concatenate([jnp.where(upper, other, held), jnp.where(upper, held, other)], axis=1)
        bit, shift = bit * 2, shift + 1
    pieces = held.reshape(-1, dim)
    order = [(0, 0)]

    def double_up(pieces, order, mask):
        other = swap(pieces, mask)
        mine = own.reshape(pieces.shape) if len(order) == 1 and not shift else pieces
        return jnp.concatenate([mine, other], axis=0), order + [(p, (mask % parts >> shift) ^ f) for p, f in order]

    for bit in [1 << k for k in range(max(1, shift), parts.bit_length() - 1)]:
        pieces, order = double_up(pieces, order, mask_of(bit))
    infos = info
    hops = [1 << k for k in reversed(range(planes.bit_length() - 1))]
    for bit in hops[:-1]:
        mask = (bit * parts) | 1
        known = infos.shape[0] // INFO
        split = pieces.shape[0]
        other = swap(jnp.concatenate([pieces, infos], axis=0), mask)
        pieces = jnp.concatenate([pieces, other[:split]], axis=0)
        infos = jnp.concatenate([infos, other[split:]], axis=0)
        order = order + [(p + known, (mask % parts >> shift) ^ f) for p, f in order]
    mask = (hops[-1] * parts) | 1
    split = pieces.shape[0]
    sent = jnp.concatenate([pieces, infos], axis=0)
    other = swap(sent, mask)
    packed, other = [sent], [other]
    flips = [(p, (mask % parts >> shift) ^ f) for p, f in order]
    if not shift:
        packed.append(swap(pieces, 1))
        other.append(swap(other[0][:split], 1))
        order = order + [(p, 1 ^ f) for p, f in order]
        flips = flips + [(p, 1 ^ f) for p, f in flips]

    columns = planes // 2 * query_count * tokens
    double = 2 if columns <= 128 else 1
    token_scratch = pltpu.VMEM((columns * double, dim * double), jnp.bfloat16)
    best_scratch = pltpu.VMEM((pages, columns), jnp.float32)
    message = jax.ShapeDtypeStruct((planes // 2, blocks, tokens // repeat, LANES), jnp.float32)

    def call(kernel, count, **kwargs):
        return pl.pallas_call(
            kernel,
            cost_estimate=pl.CostEstimate(
                flops=2 * count * patches * dim * columns, transcendentals=0, bytes_accessed=count * patches * dim * 2
            ),
            compiler_params=pltpu.CompilerParams(vmem_limit_bytes=24 << 20),
            **kwargs,
        )

    near_best = call(
        functools.partial(near_first_kernel, order, shift, len(packed)),
        last,
        out_shape=jax.ShapeDtypeStruct((last, columns), jnp.float32),
        in_specs=[VMEM] * (len(packed) + 1),
        out_specs=VMEM,
        scratch_shapes=[token_scratch],
    )(*packed, gallery_c)
    far = call(
        functools.partial(far_kernel, query_count, cand, flips, shift, len(other)),
        pages,
        out_shape=message,
        in_specs=[VMEM] * (len(packed) + 3),
        out_specs=VMEM,
        scratch_shapes=[token_scratch, best_scratch],
    )(*other, gallery_a, gallery_b, gallery_c)
    near = call(
        functools.partial(near_second_kernel, query_count, cand, order, shift, len(packed)),
        pages - last,
        out_shape=message,
        in_specs=[VMEM] * (len(packed) + 3),
        out_specs=VMEM,
        scratch_shapes=[token_scratch, best_scratch],
    )(*packed, near_best, gallery_a, gallery_b)
    for bit in reversed(hops):
        arrived = swap(far, (bit * parts) | 1)
        best = jnp.maximum(near, arrived)
        half = best.shape[0] // 2
        near, far = best[:half], best[half:]
    best = best[0]
    bit = parts // 2
    while bit > 1:
        best = jnp.maximum(best, swap(best, mask_of(bit)))
        bit //= 2
    return pl.pallas_call(
        functools.partial(finish_kernel, query_count, cand, tokens),
        out_shape=jax.ShapeDtypeStruct((query_count, cand), jnp.float32),
        in_specs=[VMEM, VMEM],
        out_specs=VMEM,
        compiler_params=pltpu.CompilerParams(vmem_limit_bytes=8 << 20),
        name="finish",
    )(best, swap(best, 1))


def solution(mesh):
    in_specs = (
        P(("groups", "pages"), "patches", None),
        P(("groups", "pages"), "patches", None),
        P("groups"),
        P(("groups", "pages"), None),
    )
    out_specs = P(("groups", "pages"), None)
    return jax.shard_map(body, mesh=mesh, in_specs=in_specs, out_specs=out_specs, check_vma=False)
```
